256 devices in a mesh: group: 8 (over z_lo, y), ctx: 32 (over x, z_hi, core).
Axes of the slice: x: 4, y: 4, z: 8 (z_hi: 4, z_lo: 2; z = z_hi * 2 + z_lo), core: 2. Of those that a mesh axis runs over, the one named last changes fastest.
Arguments:
- hidden_x: bfloat16 [8, 8192, 8192], P('group', 'ctx'), may hold values from -6 to 6
- gate_z: bfloat16 [8, 8192, 8192], P('group', 'ctx'), may hold values from -6 to 6
- lengths: int32 [8, 32], P('group', 'ctx'), may hold values from 128 to 256, as said below
- conv_weight: float32 [4, 8192], P(None, ('group', 'ctx')), may hold values from -3 to 3
- conv_bias: float32 [8192], P(('group', 'ctx')), may hold values from -3 to 3
- xproj_weight: bfloat16 [8192, 288], P(('group', 'ctx')), may hold values from -0.0625 to 0.0625
- dtproj_weight: bfloat16 [256, 8192], P(None, ('group', 'ctx')), may hold values from -0.375 to 0.375
- dt_bias: float32 [8192], P(('group', 'ctx')), may hold values from -4.6 to -2.25
- a_log: float32 [16, 8192], P(None, ('group', 'ctx')), may hold values from -8.5 to -0.7
- skip_gain: float32 [8192], P(('group', 'ctx')), may hold values from 0.5 to 2
Outputs:
- gated: bfloat16 [8, 8192, 8192], P('group', 'ctx')
The draws below stay inside these ranges and needn't reach their ends.
Inputs may be any that keep to these rules, and one draw needn't show every extreme that they name: Block c of record r holds lengths[r, c] valid positions at its start and padding after them.
All inputs are finite; a program needn't handle non-finite values.
Results may differ from the reference program's by a relative error of at most 0.0015.
The reference program's roundings to bfloat16 on the way (of `conv_act` and `dt_low`) count: a program that leaves them out, or rounds other values in their place, can miss the bound.
Values may be sent and summed in bfloat16 or wider, within the bound.
No kernel may reach another device: no remote copies, remote signals or barrier semaphores. Data moves between devices by JAX's collectives and lax.ppermute only.
A program may use at most 192 MiB of HBM per device.

```python
import jax
import jax.numpy as jnp
from jax import lax

E = 8192
N = 16
DTR = 256
KCONV = 4
TOK_DEV = 256
PROJ = 288
RECORDS = 8
SEQ = 8192
N_CTX = 32


def draw_lengths(key, part):
    count = RECORDS * N_CTX
    base = jax.random.randint(key, (count,), TOK_DEV // 2, TOK_DEV + 1)
    top_place = jax.random.randint(jax.random.fold_in(key, 11), (), 0, count)
    step_away = jax.random.randint(jax.random.fold_in(key, 12), (), 1, count)
    low_place = (top_place + step_away) % count
    base = base.at[top_place].set(TOK_DEV)
    base = base.at[low_place].set(TOK_DEV // 2)
    return base.reshape(RECORDS, N_CTX).astype(jnp.int32)


def block_levels(key, shape, cuts, low, largest):
    loudness, own = 1.0, jax.random.fold_in(key, 6)
    for axis_at, parts in cuts:
        heights = jnp.exp(jax.random.uniform(jax.random.fold_in(own, axis_at), (parts,), jnp.float32, low / len(cuts), largest / len(cuts)))
        loudness = loudness * jnp.repeat(heights, shape[axis_at] // parts).reshape([-1 if axis == axis_at else 1 for axis in range(len(shape))])
    return loudness


def bell_draw(key, shape, width, reach, cuts=(), held_as=jnp.bfloat16):
    loudness = block_levels(key, shape, cuts, -0.22, 0.18) if cuts else 1.0
    array = jax.random.normal(key, shape, jnp.float32) * width * loudness
    return jnp.minimum(jnp.maximum(array, -reach), reach).astype(held_as)


def setup_inputs(seed: int = 0) -> dict:
    keys = jax.random.split(jax.random.key(seed), 11)
    hidden_x = bell_draw(keys[0], (RECORDS, SEQ, E), 1.0, 6.0, ((0, 8), (1, 32)))
    gate_z = bell_draw(keys[1], (RECORDS, SEQ, E), 1.0, 6.0, ((0, 8), (1, 32)))
    lengths = draw_lengths(jax.random.fold_in(keys[10], 71), 0)
    conv_weight = bell_draw(keys[3], (KCONV, E), KCONV ** -0.5, 3.0, ((1, 256),), jnp.float32)
    conv_bias = bell_draw(keys[4], (E,), 0.5, 3.0, ((0, 256),), jnp.float32)
    xproj_weight = bell_draw(keys[5], (E, PROJ), E ** -0.5, 0.0625, ((0, 256),))
    dtproj_weight = bell_draw(keys[6], (DTR, E), DTR ** -0.5, 0.375, ((1, 256),))
    dt_bias = jnp.clip(-4.6 + 2.35 * jax.random.uniform(keys[7], (E,), jnp.float32) ** block_levels(keys[7], (E,), ((0, 256),), -0.2, 0.2), -4.6, -2.25)
    a_log = jnp.clip(-8.5 + 7.8 * jax.random.uniform(keys[8], (N, E), jnp.float32) ** block_levels(keys[8], (N, E), ((1, 256),), -0.2, 0.2), -8.5, -0.7)
    skip_gain = jnp.clip(0.5 + 1.5 * jax.random.uniform(keys[9], (E,), jnp.float32) ** block_levels(keys[9], (E,), ((0, 256),), -0.2, 0.2), 0.5, 2.0)
    return {"hidden_x": hidden_x, "gate_z": gate_z, "lengths": lengths, "conv_weight": conv_weight, "conv_bias": conv_bias, "xproj_weight": xproj_weight, "dtproj_weight": dtproj_weight, "dt_bias": dt_bias, "a_log": a_log, "skip_gain": skip_gain}


def reference(hidden_x, gate_z, lengths, conv_weight, conv_bias, xproj_weight, dtproj_weight, dt_bias, a_log, skip_gain):
    place = jnp.arange(SEQ, dtype=jnp.int32) % TOK_DEV
    limit = jnp.repeat(lengths, TOK_DEV, axis=1)
    valid = (place[None, :] < limit).astype(jnp.float32)
    a_matrix = -jnp.exp(a_log)

    def one_record(inputs):
        x_record, z_record, v_record = inputs
        masked = x_record.astype(jnp.float32) * v_record[:, None]
        padded = jnp.concatenate([jnp.zeros((KCONV - 1, E), jnp.float32), masked], axis=0)
        total = conv_bias[None, :] + conv_weight[0][None, :] * padded[0:SEQ]
        for offset in range(1, KCONV):
            total = total + conv_weight[offset][None, :] * padded[offset:offset + SEQ]
        conv_act = jax.nn.silu(total).astype(jnp.bfloat16)
        proj = jnp.dot(conv_act, xproj_weight, preferred_element_type=jnp.float32)
        dt_low = proj[:, :DTR].astype(jnp.bfloat16)
        b_rows = proj[:, DTR:DTR + N]
        c_rows = proj[:, DTR + N:]
        step_size = jax.nn.softplus(jnp.dot(dt_low, dtproj_weight, preferred_element_type=jnp.float32) + dt_bias[None, :]) * v_record[:, None]
        x_act = conv_act.astype(jnp.float32)

        def advance(state, row):
            x_row, d_row, b_row, c_row = row
            state = jnp.exp(a_matrix * d_row[None, :]) * state + (d_row * x_row)[None, :] * b_row[:, None]
            return state, jnp.sum(c_row[:, None] * state, axis=0)

        start = jnp.zeros((N, E), jnp.float32)
        ending, y_all = lax.scan(advance, start, (x_act, step_size, b_rows, c_rows))
        mixed = (y_all + skip_gain[None, :] * x_act) * jax.nn.silu(z_record.astype(jnp.float32)) * v_record[:, None]
        return mixed.astype(jnp.bfloat16)

    return lax.map(one_record, (hidden_x, gate_z, valid))
```

```python
import jax
import jax.numpy as jnp
from jax import lax
from jax.experimental import pallas as pl
from jax.experimental.pallas import tpu as pltpu
from jax.sharding import PartitionSpec as P

LOG2E = 1.4426950408889634
LANES = 128
ROWS = 8
WIDE = ROWS * LANES


def sigmoid(v):
    return 1.0 / (1.0 + jnp.exp(-v))


def settings():
    return pltpu.CompilerParams(dimension_semantics=("arbitrary",), vmem_limit_bytes=56 << 20)


def whole(shape):
    return pl.BlockSpec(shape, lambda i, *_: (0,) * len(shape))


def per_step(count):
    return pl.BlockSpec((count, ROWS, LANES), lambda i, *_: (0, i, 0))


def conv_kernel(len_ref, x_ref, rim_ref, par_ref, xw_ref, act_ref, proj_ref, pad_ref):
    tok, width = x_ref.shape
    keep = lax.broadcasted_iota(jnp.int32, (tok, LANES), 0) < len_ref[0]
    for g in range(width // LANES):
        cols = slice(g * LANES, (g + 1) * LANES)
        pad_ref[0:8, :] = rim_ref[:, cols].astype(jnp.float32)
        pad_ref[8 : 8 + tok, :] = jnp.where(keep, x_ref[:, cols].astype(jnp.float32), 0.0)
        total = par_ref[4, g : g + 1, :] + par_ref[0, g : g + 1, :] * pad_ref[5 : 5 + tok, :]
        for k in range(1, 4):
            total = total + par_ref[k, g : g + 1, :] * pad_ref[5 + k : 5 + k + tok, :]
        act_ref[:, cols] = (total * sigmoid(total)).astype(jnp.bfloat16)
    weight = xw_ref[...].reshape(width, xw_ref.shape[-1])
    part = jnp.dot(act_ref[...], weight, preferred_element_type=jnp.float32)

    @pl.when(pl.program_id(0) == 0)
    def _():
        proj_ref[...] = part

    @pl.when(pl.program_id(0) > 0)
    def _():
        proj_ref[...] += part


def conv_proj(length, x, rim, pars, xw):
    tok, chans = x.shape
    pieces, _, rows, cols = xw.shape
    return pl.pallas_call(
        conv_kernel,
        grid_spec=pltpu.PrefetchScalarGridSpec(
            num_scalar_prefetch=1,
            grid=(chans // WIDE,),
            in_specs=[
                pl.BlockSpec((tok, WIDE), lambda i, *_: (0, i)),
                pl.BlockSpec((8, WIDE), lambda i, *_: (0, i)),
                per_step(pars.shape[0]),
                pl.BlockSpec((pieces, 1, rows, cols), lambda i, *_: (0, i, 0, 0)),
            ],
            out_specs=[pl.BlockSpec((tok, WIDE), lambda i, *_: (0, i)), whole((tok, cols))],
            scratch_shapes=[pltpu.VMEM((tok + 8, LANES), jnp.float32)],
        ),
        out_shape=[
            jax.ShapeDtypeStruct((tok, chans), jnp.bfloat16),
            jax.ShapeDtypeStruct((tok, cols), jnp.float32),
        ],
        compiler_params=settings(),
        name="conv_proj",
    )(length, x, rim, pars, xw)


def scan_kernel(
    len_ref, low_ref, dw_ref, par_ref, alog_ref, act_ref, b_ref, c_ref,
    y_ref, cum_ref, end_ref, d_scr, x_scr, a_scr,
):
    tok, rank = low_ref.shape
    states = alog_ref.shape[0]
    keep = lax.broadcasted_iota(jnp.int32, (tok, LANES), 0) < len_ref[0]
    raw = lax.dot_general(
        low_ref[...],
        dw_ref[...].reshape(WIDE, rank),
        (((1,), (1,)), ((), ())),
        preferred_element_type=jnp.float32,
    )
    for g in range(ROWS):
        cols = slice(g * LANES, (g + 1) * LANES)
        v = raw[:, cols] + par_ref[5, g : g + 1, :]
        soft = jnp.maximum(v, 0.0) + jnp.log1p(jnp.exp(-jnp.abs(v)))
        d = jnp.where(keep, soft, 0.0)
        place = slice(g * 8, (g + 1) * 8)
        d_scr[:, place, :] = d.reshape(tok // 8, 8, LANES)
        x_scr[:, place, :] = (d * act_ref[:, cols].astype(jnp.float32)).reshape(tok // 8, 8, LANES)
    a_scr[...] = jnp.exp(alog_ref[...]) * (-LOG2E)

    def block(i, carry):
        hs, cum = carry
        hs = list(hs)
        for o in range(16):
            t = i * 16 + o
            tile = i * 2 + o // 8
            d = d_scr[tile, pl.ds(o % 8, ROWS, stride=8), :]
            dx = x_scr[tile, pl.ds(o % 8, ROWS, stride=8), :]
            cum = cum + d
            acc = [None] * 4
            for n in range(states):
                b = b_ref[pl.ds(t * states + n, ROWS, stride=0), :]
                c = c_ref[pl.ds(t * states + n, ROWS, stride=0), :]
                hs[n] = jnp.exp2(a_scr[n] * d) * hs[n] + dx * b
                term = c * hs[n]
                acc[n % 4] = term if acc[n % 4] is None else acc[n % 4] + term
            y_ref[t] = (acc[0] + acc[1]) + (acc[2] + acc[3])
            cum_ref[t] = cum
        return tuple(hs), cum

    zero = jnp.zeros((ROWS, LANES), jnp.float32)
    hs, cum = lax.fori_loop(0, tok // 16, block, ((zero,) * states, zero))
    for q in range(ROWS // 2):
        pair = slice(2 * q, 2 * q + 2)
        for n in range(states):
            end_ref[q, 2 * n : 2 * n + 2, :] = hs[n][pair]
        for k in range(4):
            at = 2 * states + 2 * k
            end_ref[q, at : at + 2, :] = cum[pair]


def scan_pass(length, low, dw, pars, alog, act, b_wide, c_wide):
    tok, chans = act.shape
    pieces, _, rows, rank = dw.shape
    states = alog.shape[0]
    groups = chans // LANES
    sent = 2 * states + 8
    return pl.pallas_call(
        scan_kernel,
        grid_spec=pltpu.PrefetchScalarGridSpec(
            num_scalar_prefetch=1,
            grid=(chans // WIDE,),
            in_specs=[
                whole((tok, rank)),
                pl.BlockSpec((pieces, 1, rows, rank), lambda i, *_: (0, i, 0, 0)),
                per_step(pars.shape[0]),
                per_step(states),
                pl.BlockSpec((tok, WIDE), lambda i, *_: (0, i)),
                whole((tok * states, LANES)),
                whole((tok * states, LANES)),
            ],
            out_specs=[
                per_step(tok),
                per_step(tok),
                pl.BlockSpec((ROWS // 2, sent, LANES), lambda i, *_: (i, 0, 0)),
            ],
            scratch_shapes=[
                pltpu.VMEM((tok // 8, 8 * ROWS, LANES), jnp.float32),
                pltpu.VMEM((tok // 8, 8 * ROWS, LANES), jnp.float32),
                pltpu.VMEM((states, ROWS, LANES), jnp.float32),
            ],
        ),
        out_shape=[
            jax.ShapeDtypeStruct((tok, groups, LANES), jnp.float32),
            jax.ShapeDtypeStruct((tok, groups, LANES), jnp.float32),
            jax.ShapeDtypeStruct((groups // 2, sent, LANES), jnp.float32),
        ],
        compiler_params=settings(),
        name="scan_pass",
    )(length, low, dw, pars, alog, act, b_wide, c_wide)


def prefix_kernel(end_ref, alog_ref, in_ref):
    blocks = end_ref.shape[0]
    rows = alog_ref.shape[0]
    a = [jnp.exp(alog_ref[r : r + 8, :]) * (-LOG2E) for r in range(0, rows, 8)]
    hs = [jnp.zeros((8, LANES), jnp.float32) for _ in a]
    for k in range(blocks):
        spent = end_ref[k, rows : rows + 8, :]
        for j in range(len(a)):
            in_ref[k, 8 * j : 8 * j + 8, :] = hs[j]
            hs[j] = jnp.exp2(a[j] * spent) * hs[j] + end_ref[k, 8 * j : 8 * j + 8, :]


def prefix(ends, alog):
    return pl.pallas_call(
        prefix_kernel,
        out_shape=jax.ShapeDtypeStruct((ends.shape[0], *alog.shape), jnp.float32),
        name="prefix",
    )(ends, alog)


def gate_kernel(
    len_ref, y_ref, cum_ref, hin_ref, par_ref, alog_ref, act_ref, z_ref, c_ref,
    out_ref, y_scr, a_scr, h_scr,
):
    tok = act_ref.shape[0]
    states = alog_ref.shape[0]
    a_scr[...] = jnp.exp(alog_ref[...]) * (-LOG2E)
    for q in range(ROWS // 2):
        for n in range(states):
            h_scr[n, 2 * q : 2 * q + 2, :] = hin_ref[q, 2 * n : 2 * n + 2, :]

    def block(i, carry):
        for o in range(8):
            t = i * 8 + o
            cum = cum_ref[t]
            acc = [y_ref[t]] + [None] * 3
            for n in range(states):
                c = c_ref[pl.ds(t * states + n, ROWS, stride=0), :]
                term = (c * h_scr[n]) * jnp.exp2(a_scr[n] * cum)
                acc[n % 4] = term if acc[n % 4] is None else acc[n % 4] + term
            y_scr[i, pl.ds(o, ROWS, stride=8), :] = (acc[0] + acc[1]) + (acc[2] + acc[3])
        return carry

    lax.fori_loop(0, tok // 8, block, 0)
    keep = lax.broadcasted_iota(jnp.int32, (tok, LANES), 0) < len_ref[0]
    for g in range(ROWS):
        cols = slice(g * LANES, (g + 1) * LANES)
        y = y_scr[:, g * 8 : (g + 1) * 8, :].reshape(tok, LANES)
        z = z_ref[:, cols].astype(jnp.float32)
        out = (y + par_ref[6, g : g + 1, :] * act_ref[:, cols].astype(jnp.float32)) * (z * sigmoid(z))
        out_ref[:, cols] = jnp.where(keep, out, 0.0).astype(jnp.bfloat16)


def gate_pass(length, y, cum, hin, pars, alog, act, z, c_wide):
    tok, chans = act.shape
    states = alog.shape[0]
    return pl.pallas_call(
        gate_kernel,
        grid_spec=pltpu.PrefetchScalarGridSpec(
            num_scalar_prefetch=1,
            grid=(chans // WIDE,),
            in_specs=[
                per_step(tok),
                per_step(tok),
                pl.BlockSpec((ROWS // 2, 2 * states, LANES), lambda i, *_: (i, 0, 0)),
                per_step(pars.shape[0]),
                per_step(states),
                pl.BlockSpec((tok, WIDE), lambda i, *_: (0, i)),
                pl.BlockSpec((tok, WIDE), lambda i, *_: (0, i)),
                whole((tok * states, LANES)),
            ],
            out_specs=pl.BlockSpec((tok, WIDE), lambda i, *_: (0, i)),
            scratch_shapes=[
                pltpu.VMEM((tok // 8, 8 * ROWS, LANES), jnp.float32),
                pltpu.VMEM((states, ROWS, LANES), jnp.float32),
                pltpu.VMEM((states, ROWS, LANES), jnp.float32),
            ],
        ),
        out_shape=jax.ShapeDtypeStruct((tok, chans), jnp.bfloat16),
        compiler_params=settings(),
        name="gate_pass",
    )(length, y, cum, hin, pars, alog, act, z, c_wide)


def everywhere(shard):
    return lax.all_gather(lax.all_gather(shard, "group"), "ctx")


def shards(
    hidden_x, gate_z, lengths, conv_weight, conv_bias, xproj_weight, dtproj_weight, dt_bias, a_log, skip_gain
):
    x, z = hidden_x[0], gate_z[0]
    tok, chans = x.shape
    taps = conv_weight.shape[0]
    rank = dtproj_weight.shape[0]
    states = a_log.shape[0]
    blocks = lax.axis_size("ctx")
    length = lengths[0]

    small = jnp.concatenate(
        [conv_weight, conv_bias[None], dt_bias[None], skip_gain[None], a_log], axis=0
    )
    small = everywhere(small)
    small = small.reshape(8, 4, *small.shape[1:]).transpose(3, 2, 0, 1, 4)
    small = small.reshape(small.shape[0], chans // LANES, LANES)
    pars, alog = small[: taps + 3], small[taps + 3 :]
    xw = everywhere(xproj_weight)
    dw = everywhere(dtproj_weight.T)

    edge = jnp.arange(tok - (taps - 1), tok, dtype=jnp.int32)[:, None] < length
    edge = jnp.where(edge, x[tok - (taps - 1) :], jnp.bfloat16(0))
    rim = lax.ppermute(edge, "ctx", [(i, i + 1) for i in range(blocks - 1)])
    rim = jnp.concatenate([jnp.zeros((8 - (taps - 1), chans), x.dtype), rim], axis=0)

    act, proj = conv_proj(length, x, rim, pars, xw)
    low = proj[:, :rank].astype(jnp.bfloat16)
    b_wide = jnp.broadcast_to(proj[:, rank : rank + states].reshape(-1, 1), (tok * states, LANES))
    c_wide = jnp.broadcast_to(proj[:, rank + states :].reshape(-1, 1), (tok * states, LANES))
    y, cum, ends = scan_pass(length, low, dw, pars, alog, act, b_wide, c_wide)

    own = 2 * lax.axis_index("ctx")
    mine = lax.dynamic_slice_in_dim(alog, own, 2, axis=1).reshape(2 * states, LANES)
    ends = lax.all_to_all(ends, "ctx", split_axis=0, concat_axis=0, tiled=True)
    hin = prefix(ends, mine)
    hin = lax.all_to_all(hin, "ctx", split_axis=0, concat_axis=0, tiled=True)
    out = gate_pass(length, y, cum, hin, pars, alog, act, z, c_wide)
    return out[None]


def solution(mesh):
    spread = ("group", "ctx")
    in_specs = (
        P("group", "ctx", None),
        P("group", "ctx", None),
        P("group", "ctx"),
        P(None, spread),
        P(spread),
        P(spread, None),
        P(None, spread),
        P(spread),
        P(None, spread),
        P(spread),
    )
    return jax.shard_map(
        shards, mesh=mesh, in_specs=in_specs, out_specs=P("group", "ctx", None), check_vma=False
    )
```

```python
import jax
import jax.numpy as jnp
from jax import lax
from jax.experimental import pallas as pl
from jax.experimental.pallas import tpu as pltpu
from jax.sharding import PartitionSpec as P

LOG2E = 1.4426950408889634
LANES = 128
ROWS = 8
VECTORS = 7
WIDE = ROWS * LANES


def sigmoid(v):
    return 1.0 / (1.0 + jnp.exp(-v))


def settings():
    return pltpu.CompilerParams(dimension_semantics=("arbitrary",), vmem_limit_bytes=56 << 20)


def whole(shape):
    return pl.BlockSpec(shape, lambda i, *_: (0,) * len(shape))


def per_step(count):
    return pl.BlockSpec((count, ROWS, LANES), lambda i, *_: (0, i, 0))


def conv_kernel(len_ref, x_ref, rim_ref, raw_ref, act_ref, par_ref, pad_ref):
    tok, width = x_ref.shape
    quarter = LANES // 4
    spot = lax.broadcasted_iota(jnp.int32, (ROWS, LANES), 1) // quarter
    for r in range(par_ref.shape[0] // 4):
        rows = [raw_ref[pl.ds(q * 64 + r, ROWS, stride=8), :] for q in range(4)]
        for j in range(4):
            turned = [rows[q] if q == j else pltpu.roll(rows[q], ((q - j) % 4) * quarter, 1) for q in range(4)]
            low = jnp.where(spot == 0, turned[0], turned[1])
            high = jnp.where(spot == 2, turned[2], turned[3])
            par_ref[4 * r + j] = jnp.where(spot < 2, low, high)
    keep = lax.broadcasted_iota(jnp.int32, (tok, LANES), 0) < len_ref[0]
    for g in range(width // LANES):
        cols = slice(g * LANES, (g + 1) * LANES)
        pad_ref[0:8, :] = rim_ref[:, cols].astype(jnp.float32)
        pad_ref[8 : 8 + tok, :] = jnp.where(keep, x_ref[:, cols].astype(jnp.float32), 0.0)
        total = par_ref[4, g : g + 1, :] + par_ref[0, g : g + 1, :] * pad_ref[5 : 5 + tok, :]
        for k in range(1, 4):
            total = total + par_ref[k, g : g + 1, :] * pad_ref[5 + k : 5 + k + tok, :]
        act_ref[:, cols] = (total * sigmoid(total)).astype(jnp.bfloat16)


def convolve(length, x, rim, raw, count):
    tok, chans = x.shape
    return pl.pallas_call(
        conv_kernel,
        grid_spec=pltpu.PrefetchScalarGridSpec(
            num_scalar_prefetch=1,
            grid=(chans // WIDE,),
            in_specs=[
                pl.BlockSpec((tok, WIDE), lambda i, *_: (0, i)),
                pl.BlockSpec((8, WIDE), lambda i, *_: (0, i)),
                pl.BlockSpec((256, LANES), lambda i, *_: (i, 0)),
            ],
            out_specs=[pl.BlockSpec((tok, WIDE), lambda i, *_: (0, i)), per_step(count)],
            scratch_shapes=[pltpu.VMEM((tok + 8, LANES), jnp.float32)],
        ),
        out_shape=[
            jax.ShapeDtypeStruct((tok, chans), jnp.bfloat16),
            jax.ShapeDtypeStruct((count, chans // LANES, LANES), jnp.float32),
        ],
        compiler_params=settings(),
        name="convolve",
    )(length, x, rim, raw)


def piece_specs(pieces):
    specs = []
    for k, p in enumerate(pieces):
        rest = (p.shape[1], p.shape[2], 1, *p.shape[4:])
        if k < len(pieces) // 2:
            specs.append(
                pl.BlockSpec((1, *rest), lambda i, s: ((jnp.minimum(i, 7) - s[2]) & 3, 0, 0, jnp.minimum(i, 7) // 4, 0, 0))
            )
        else:
            specs.append(pl.BlockSpec((4, *rest), lambda i, s: (0, 0, 0, jnp.minimum(i, 7) // 4, 0, 0)))
    return specs


def assemble(step, info_ref, piece_refs, w_ref):
    own_x, own_y, own_core = info_ref[1], info_ref[2], info_ref[3]
    half = piece_refs[0].shape[4]
    many = len(piece_refs) // 2
    ahead = 1 + 2 * own_core
    away = (0, ahead, 4 - ahead, 2, 2)
    first = (0, 0, 0, own_core, 1 - own_core)
    for j, ref in enumerate(piece_refs[:many]):
        at = (own_x + away[j]) & 3
        for core in range(ref.shape[1]):
            for h in range(ref.shape[2]):
                w_ref[at, h, first[j] + core, 0:half, :] = ref[0, core, h, 0]
    wanted = (step - own_y) & 3
    for j, ref in enumerate(piece_refs[many:]):

        @pl.when(wanted == away[j])
        def _(ref=ref, first=first[j]):
            for q in range(4):
                for core in range(ref.shape[1]):
                    for h in range(ref.shape[2]):
                        w_ref[(own_x + q) & 3, h, first + core, half : 2 * half, :] = ref[q, core, h, 0]


def scan_kernel(info_ref, par_ref, act_ref, *refs):
    *piece_refs, y_ref, cum_ref, end_ref, c_ref, sum_scr, low_scr, b_scr, act_scr, d_scr, x_scr, a_scr, w_scr = refs
    step = pl.program_id(0)
    many = act_scr.shape[0]
    tok, rank = low_scr.shape
    states = a_scr.shape[0]

    @pl.when(step < many)
    def _():
        assemble(step, info_ref, piece_refs, w_scr.at[step])
        weight = w_scr[step].reshape(WIDE, w_scr.shape[-1])[:, : sum_scr.shape[1]]
        act_scr[step] = act_ref[...]
        part = jnp.dot(act_ref[...], weight, preferred_element_type=jnp.float32)

        @pl.when(step == 0)
        def _():
            sum_scr[...] = part

        @pl.when(step > 0)
        def _():
            sum_scr[...] += part

        @pl.when(step == many - 1)
        def _():
            low_scr[...] = sum_scr[:, :rank].astype(jnp.bfloat16)
            for n in range(states):
                for ref, col in ((b_scr, rank + n), (c_ref, rank + states + n)):
                    ref[n * tok : (n + 1) * tok, :] = jnp.broadcast_to(sum_scr[:, col : col + 1], (tok, LANES))

    @pl.when(step >= many)
    def _():
        at = step - many
        keep = lax.broadcasted_iota(jnp.int32, (tok, LANES), 0) < info_ref[0]
        raw = lax.dot_general(
            low_scr[...],
            w_scr[at].reshape(WIDE, w_scr.shape[-1])[:, w_scr.shape[-1] - rank :],
            (((1,), (1,)), ((), ())),
            preferred_element_type=jnp.float32,
        )
        for g in range(ROWS):
            cols = slice(g * LANES, (g + 1) * LANES)
            v = raw[:, cols] + par_ref[5, g : g + 1, :]
            soft = jnp.maximum(v, 0.0) + jnp.log1p(jnp.exp(-jnp.abs(v)))
            d = jnp.where(keep, soft, 0.0)
            place = slice(g * 8, (g + 1) * 8)
            d_scr[:, place, :] = d.reshape(tok // 8, 8, LANES)
            dx = d * act_scr[at, :, cols].astype(jnp.float32)
            x_scr[:, place, :] = dx.reshape(tok // 8, 8, LANES)
        a_scr[...] = jnp.exp(par_ref[VECTORS : VECTORS + states]) * (-LOG2E)

        def block(i, carry):
            hs, cum = carry
            hs = list(hs)
            for o in range(16):
                t = i * 16 + o
                tile = i * 2 + o // 8
                d = d_scr[tile, pl.ds(o % 8, ROWS, stride=8), :]
                dx = x_scr[tile, pl.ds(o % 8, ROWS, stride=8), :]
                cum = cum + d
                acc = [None] * 4
                for n in range(states):
                    b = b_scr[pl.ds(n * tok + t, ROWS, stride=0), :]
                    c = c_ref[pl.ds(n * tok + t, ROWS, stride=0), :]
                    hs[n] = jnp.exp2(a_scr[n] * d) * hs[n] + dx * b
                    term = c * hs[n]
                    acc[n % 4] = term if acc[n % 4] is None else acc[n % 4] + term
                y_ref[t] = (acc[0] + acc[1]) + (acc[2] + acc[3])
                cum_ref[t] = cum
            return tuple(hs), cum

        zero = jnp.zeros((ROWS, LANES), jnp.float32)
        hs, cum = lax.fori_loop(0, tok // 16, block, ((zero,) * states, zero))
        for q in range(ROWS // 2):
            pair = slice(2 * q, 2 * q + 2)
            for n in range(states):
                end_ref[q, 2 * n : 2 * n + 2, :] = hs[n][pair]
            for k in range(4):
                row = 2 * states + 2 * k
                end_ref[q, row : row + 2, :] = cum[pair]


def scan_pass(info, pars, act, pieces, rank, states):
    tok, chans = act.shape
    rows, cols = pieces[0].shape[4:]
    many = chans // WIDE
    groups = chans // LANES
    sent = 2 * states + 8

    def turn(shape, where):
        def index(i, s):
            later = jnp.maximum(i - many, 0)
            return (0,) * where + (later,) + (0,) * (len(shape) - 1 - where)

        return pl.BlockSpec(shape, index)

    return pl.pallas_call(
        scan_kernel,
        grid_spec=pltpu.PrefetchScalarGridSpec(
            num_scalar_prefetch=1,
            grid=(2 * many,),
            in_specs=[
                turn((pars.shape[0], ROWS, LANES), 1),
                pl.BlockSpec((tok, WIDE), lambda i, s: (0, jnp.minimum(i, many - 1))),
                *piece_specs(pieces),
            ],
            out_specs=[
                turn((tok, ROWS, LANES), 1),
                turn((tok, ROWS, LANES), 1),
                turn((ROWS // 2, sent, LANES), 0),
                whole((tok * states, LANES)),
            ],
            scratch_shapes=[
                pltpu.VMEM((tok, cols - rank), jnp.float32),
                pltpu.VMEM((tok, rank), jnp.bfloat16),
                pltpu.VMEM((tok * states, LANES), jnp.float32),
                pltpu.VMEM((many, tok, WIDE), jnp.bfloat16),
                pltpu.VMEM((tok // 8, 8 * ROWS, LANES), jnp.float32),
                pltpu.VMEM((tok // 8, 8 * ROWS, LANES), jnp.float32),
                pltpu.VMEM((states, ROWS, LANES), jnp.float32),
                pltpu.VMEM((many, 4, 4, 2, 2 * rows, cols), jnp.bfloat16),
            ],
        ),
        out_shape=[
            jax.ShapeDtypeStruct((tok, groups, LANES), jnp.float32),
            jax.ShapeDtypeStruct((tok, groups, LANES), jnp.float32),
            jax.ShapeDtypeStruct((groups // 2, sent, LANES), jnp.float32),
            jax.ShapeDtypeStruct((tok * states, LANES), jnp.float32),
        ],
        compiler_params=settings(),
        name="scan_pass",
    )(info, pars, act, *pieces)


def prefix_kernel(end_ref, alog_ref, in_ref):
    blocks = end_ref.shape[0]
    rows = alog_ref.shape[0]
    a = [jnp.exp(alog_ref[r : r + 8, :]) * (-LOG2E) for r in range(0, rows, 8)]
    hs = [jnp.zeros((8, LANES), jnp.float32) for _ in a]
    for k in range(blocks):
        spent = end_ref[k, rows : rows + 8, :]
        for j in range(len(a)):
            in_ref[k, 8 * j : 8 * j + 8, :] = hs[j]
            hs[j] = jnp.exp2(a[j] * spent) * hs[j] + end_ref[k, 8 * j : 8 * j + 8, :]


def prefix(ends, alog):
    return pl.pallas_call(
        prefix_kernel,
        out_shape=jax.ShapeDtypeStruct((ends.shape[0], *alog.shape), jnp.float32),
        name="prefix",
    )(ends, alog)


def gate_kernel(len_ref, y_ref, cum_ref, hin_ref, par_ref, act_ref, z_ref, c_ref, out_ref, y_scr, a_scr, h_scr):
    tok = act_ref.shape[0]
    states = a_scr.shape[0]
    a_scr[...] = jnp.exp(par_ref[VECTORS : VECTORS + states]) * (-LOG2E)
    for q in range(ROWS // 2):
        for n in range(states):
            h_scr[n, 2 * q : 2 * q + 2, :] = hin_ref[q, 2 * n : 2 * n + 2, :]

    def block(i, carry):
        for o in range(8):
            t = i * 8 + o
            cum = cum_ref[t]
            acc = [y_ref[t]] + [None] * 3
            for n in range(states):
                c = c_ref[pl.ds(n * tok + t, ROWS, stride=0), :]
                term = (c * h_scr[n]) * jnp.exp2(a_scr[n] * cum)
                acc[n % 4] = term if acc[n % 4] is None else acc[n % 4] + term
            y_scr[i, pl.ds(o, ROWS, stride=8), :] = (acc[0] + acc[1]) + (acc[2] + acc[3])
        return carry

    lax.fori_loop(0, tok // 8, block, 0)
    keep = lax.broadcasted_iota(jnp.int32, (tok, LANES), 0) < len_ref[0]
    for g in range(ROWS):
        cols = slice(g * LANES, (g + 1) * LANES)
        y = y_scr[:, g * 8 : (g + 1) * 8, :].reshape(tok, LANES)
        z = z_ref[:, cols].astype(jnp.float32)
        out = (y + par_ref[6, g : g + 1, :] * act_ref[:, cols].astype(jnp.float32)) * (z * sigmoid(z))
        out_ref[:, cols] = jnp.where(keep, out, 0.0).astype(jnp.bfloat16)


def gate_pass(info, y, cum, hin, pars, act, z, c_wide):
    tok, chans = act.shape
    states = c_wide.shape[0] // tok
    columns = pl.BlockSpec((tok, WIDE), lambda i, *_: (0, i))
    return pl.pallas_call(
        gate_kernel,
        grid_spec=pltpu.PrefetchScalarGridSpec(
            num_scalar_prefetch=1,
            grid=(chans // WIDE,),
            in_specs=[
                per_step(tok),
                per_step(tok),
                pl.BlockSpec((ROWS // 2, 2 * states, LANES), lambda i, *_: (i, 0, 0)),
                per_step(pars.shape[0]),
                columns,
                columns,
                whole((tok * states, LANES)),
            ],
            out_specs=columns,
            scratch_shapes=[
                pltpu.VMEM((tok // 8, 8 * ROWS, LANES), jnp.float32),
                pltpu.VMEM((states, ROWS, LANES), jnp.float32),
                pltpu.VMEM((states, ROWS, LANES), jnp.float32),
            ],
        ),
        out_shape=jax.ShapeDtypeStruct((tok, chans), jnp.bfloat16),
        compiler_params=settings(),
        name="gate_pass",
    )(info, y, cum, hin, pars, act, z, c_wide)


def device(x, y, z, core):
    return ((z & 1) * 4 + y) * 32 + x * 8 + (z >> 1) * 2 + core


def fetch(value, move):
    route = []
    for x in range(4):
        for y in range(4):
            for z in range(8):
                for core in range(2):
                    route.append((device(*move(x, y, z, core)), device(x, y, z, core)))
    return lax.ppermute(value, ("group", "ctx"), route)


def onward(axis):
    def move(x, y, z, core):
        step = 1 - 2 * core
        return ((x + step) % 4, y, z, core) if axis == "x" else (x, (y + step) % 4, z, core)

    return move


def flip(axis, bit):
    def move(x, y, z, core):
        return x ^ (bit if axis == "x" else 0), y ^ (bit if axis == "y" else 0), z ^ (bit if axis == "z" else 0), core ^ (
            bit if axis == "core" else 0
        )

    return move


def double(value, axis, bit, own):
    other = fetch(value, flip(axis, bit))
    low = (own & bit) == 0
    return jnp.concatenate([jnp.where(low, value, other), jnp.where(low, other, value)], axis=0)


def farther(near, axis, own_core):
    return fetch(jnp.where(own_core == 0, near[:, :1], near[:, 1:]), onward(axis))


def swap(value):
    return fetch(value, flip("core", 1))


def row_of_four(value, axis, own_core):
    near = fetch(value, onward(axis))
    far = farther(near, axis, own_core)
    near_too, far_too = swap(near), swap(far)
    zero = own_core == 0
    far = jnp.concatenate([jnp.where(zero, far, far_too), jnp.where(zero, far_too, far)], axis=1)
    return jnp.concatenate([value, jnp.where(zero, near, near_too), far, jnp.where(zero, near_too, near)], axis=0)


def shards(
    hidden_x, gate_z, lengths, conv_weight, conv_bias, xproj_weight, dtproj_weight, dt_bias, a_log, skip_gain
):
    x, z = hidden_x[0], gate_z[0]
    tok, chans = x.shape
    taps = conv_weight.shape[0]
    rank = dtproj_weight.shape[0]
    states = a_log.shape[0]
    blocks = lax.axis_size("ctx")
    length = lengths[0]
    group, ctx = lax.axis_index("group"), lax.axis_index("ctx")
    own_x, own_y, own_core = ctx >> 3, group & 3, ctx & 1
    own_z = ((ctx >> 1) & 3) * 2 + (group >> 2)
    own = {"x": own_x, "y": own_y, "z": own_z, "core": own_core}
    info = jnp.stack([lengths[0, 0], own_x, own_y, own_core]).astype(jnp.int32)

    edge = jnp.arange(tok - (taps - 1), tok, dtype=jnp.int32)[:, None] < length
    edge = jnp.where(edge, x[tok - (taps - 1) :], jnp.bfloat16(0))
    rim = lax.ppermute(edge, "ctx", [(i, i + 1) for i in range(blocks - 1)])
    rim = jnp.concatenate([jnp.zeros((8 - (taps - 1), chans), x.dtype), rim], axis=0)

    small = jnp.concatenate(
        [conv_weight, conv_bias[None], dt_bias[None], skip_gain[None], a_log, a_log[:1]], axis=0
    )
    width = small.shape[1]
    count = small.shape[0]
    small = small.reshape(1, count // 4, 4 * width)
    small = jnp.pad(small, ((0, 0), (0, 8 - count // 4), (0, 0)))
    for axis, bit in (("z", 4), ("x", 1), ("x", 2), ("core", 1), ("z", 2), ("y", 1), ("y", 2), ("z", 1)):
        small = double(small, axis, bit, own[axis])
    small = small.reshape(-1, LANES)

    fill = -(xproj_weight.shape[1] + rank) % LANES
    mats = jnp.concatenate(
        [xproj_weight, jnp.zeros((width, fill), xproj_weight.dtype), dtproj_weight.T], axis=1
    )[None]
    for axis, bit in (("z", 1), ("z", 2), ("z", 4), ("core", 1)):
        mats = double(mats, axis, bit, own[axis])
    mats = mats.reshape(1, 2, 4, 2, *mats.shape[1:])
    upper = row_of_four(mats[..., : width // 2, :], "y", own_core)
    lower = row_of_four(mats[..., width // 2 :, :], "x", own_core)
    near_x, near_y = fetch(upper, onward("x")), fetch(lower, onward("y"))
    act, pars = convolve(length, x, rim, small, count)
    near_x, near_y, act = lax.optimization_barrier((near_x, near_y, act))
    pieces = []
    for value, near, axis in ((upper, near_x, "x"), (lower, near_y, "y")):
        far = farther(near, axis, own_core)
        pieces += [value, near, swap(near), far, swap(far)]

    y, cum, ends, c_wide = scan_pass(info, pars, act, pieces, rank, states)
    mine = lax.dynamic_slice_in_dim(pars[VECTORS : VECTORS + states], 2 * ctx, 2, axis=1).reshape(2 * states, LANES)
    ends = lax.all_to_all(ends, "ctx", split_axis=0, concat_axis=0, tiled=True)
    hin = prefix(ends, mine)
    hin = lax.all_to_all(hin, "ctx", split_axis=0, concat_axis=0, tiled=True)
    out = gate_pass(info, y, cum, hin, pars, act, z, c_wide)
    return out[None]


def solution(mesh):
    spread = ("group", "ctx")
    in_specs = (
        P("group", "ctx", None),
        P("group", "ctx", None),
        P("group", "ctx"),
        P(None, spread),
        P(spread),
        P(spread, None),
        P(None, spread),
        P(spread),
        P(None, spread),
        P(spread),
    )
    return jax.shard_map(
        shards, mesh=mesh, in_specs=in_specs, out_specs=P("group", "ctx", None), check_vma=False
    )
```

```python
import jax
import jax.numpy as jnp
from jax import lax
from jax.experimental import pallas as pl
from jax.experimental.pallas import tpu as pltpu
from jax.sharding import PartitionSpec as P

LOG2E = 1.4426950408889634
LANES = 128
ROWS = 8
VECTORS = 7
WIDE = ROWS * LANES


def sigmoid(v):
    return 1.0 / (1.0 + jnp.exp(-v))


def settings():
    return pltpu.CompilerParams(dimension_semantics=("arbitrary",), vmem_limit_bytes=56 << 20)


def whole(shape):
    return pl.BlockSpec(shape, lambda i, *_: (0,) * len(shape))


def per_step(count):
    return pl.BlockSpec((count, ROWS, LANES), lambda i, *_: (0, i, 0))


def piece_specs(pieces):
    specs = []
    for k, p in enumerate(pieces):
        rest = (p.shape[1], p.shape[2], 1, *p.shape[4:])
        if k < len(pieces) // 2:
            specs.append(
                pl.BlockSpec((1, *rest), lambda i, s: ((jnp.minimum(i, 7) - s[2]) & 3, 0, 0, jnp.minimum(i, 7) // 4, 0, 0))
            )
        else:
            specs.append(pl.BlockSpec((4, *rest), lambda i, s: (0, 0, 0, jnp.minimum(i, 7) // 4, 0, 0)))
    return specs


def assemble(step, info_ref, piece_refs, w_ref):
    own_x, own_y, own_core = info_ref[1], info_ref[2], info_ref[3]
    half = piece_refs[0].shape[4]
    many = len(piece_refs) // 2
    ahead = 1 + 2 * own_core
    away = (0, ahead, 4 - ahead, 2, 2)
    first = (0, 0, 0, own_core, 1 - own_core)
    for j, ref in enumerate(piece_refs[:many]):
        at = (own_x + away[j]) & 3
        for core in range(ref.shape[1]):
            for h in range(ref.shape[2]):
                w_ref[at, h, first[j] + core, 0:half, :] = ref[0, core, h, 0]
    wanted = (step - own_y) & 3
    for j, ref in enumerate(piece_refs[many:]):

        @pl.when(wanted == away[j])
        def _(ref=ref, first=first[j]):
            for q in range(4):
                for core in range(ref.shape[1]):
                    for h in range(ref.shape[2]):
                        w_ref[(own_x + q) & 3, h, first + core, half : 2 * half, :] = ref[q, core, h, 0]


def scan_kernel(info_ref, x_ref, rim_ref, *refs):
    *piece_refs, act_ref, par_ref, y_ref, cum_ref, end_ref, c_ref = refs[:-10]
    sum_scr, low_scr, b_scr, act_scr, par_scr, pad_scr, d_scr, x_scr, a_scr, w_scr = refs[-10:]
    step = pl.program_id(0)
    many = act_scr.shape[0]
    tok, rank = low_scr.shape
    states = a_scr.shape[0]
    keep = lax.broadcasted_iota(jnp.int32, (tok, LANES), 0) < info_ref[0]

    @pl.when(step < many)
    def _():
        assemble(step, info_ref, piece_refs, w_scr.at[step])
        count = par_scr.shape[1] // ROWS
        after = rank + 2 * states
        for g in range(ROWS):
            cols = slice(g * LANES, (g + 1) * LANES)
            beside = w_scr[step, g // 2, 2 * (g % 2) : 2 * (g % 2) + 2].reshape(LANES, w_scr.shape[-1])
            beside = beside[:, after - after % LANES : after - after % LANES + LANES].astype(jnp.float32).T
            at = after % LANES
            parts = [beside[at + k * count : at + (k + 1) * count] for k in range(3)]
            vectors = (parts[0] + parts[1]) + parts[2]
            par_scr[step, pl.ds(g, count, stride=ROWS), :] = vectors
            par_ref[:, g, :] = vectors
            pad = jnp.concatenate(
                [rim_ref[:, cols].astype(jnp.float32), jnp.where(keep, x_ref[:, cols].astype(jnp.float32), 0.0)], axis=0
            )
            pad_scr[g % 2] = pad
            total = vectors[4:5] + vectors[0:1] * pad_scr[g % 2, 5 : 5 + tok, :]
            for k in range(1, 4):
                total = total + vectors[k : k + 1] * pad_scr[g % 2, 5 + k : 5 + k + tok, :]
            act = (total * sigmoid(total)).astype(jnp.bfloat16)
            act_ref[:, cols] = act
            act_scr[step, :, cols] = act
        weight = w_scr[step].reshape(WIDE, w_scr.shape[-1])[:, : sum_scr.shape[1]]
        part = jnp.dot(act_scr[step], weight, preferred_element_type=jnp.float32)

        @pl.when(step == 0)
        def _():
            sum_scr[...] = part

        @pl.when(step > 0)
        def _():
            sum_scr[...] += part

        @pl.when(step == many - 1)
        def _():
            low_scr[...] = sum_scr[:, :rank].astype(jnp.bfloat16)
            for n in range(states):
                for ref, col in ((b_scr, rank + n), (c_ref, rank + states + n)):
                    ref[n * tok : (n + 1) * tok, :] = jnp.broadcast_to(sum_scr[:, col : col + 1], (tok, LANES))

    @pl.when(step >= many)
    def _():
        at = step - many
        raw = lax.dot_general(
            low_scr[...],
            w_scr[at].reshape(WIDE, w_scr.shape[-1])[:, w_scr.shape[-1] - rank :],
            (((1,), (1,)), ((), ())),
            preferred_element_type=jnp.float32,
        )
        for g in range(ROWS):
            cols = slice(g * LANES, (g + 1) * LANES)
            v = raw[:, cols] + par_scr[at, 5 * ROWS + g : 5 * ROWS + g + 1, :]
            soft = jnp.maximum(v, 0.0) + jnp.log1p(jnp.exp(-jnp.abs(v)))
            d = jnp.where(keep, soft, 0.0)
            place = slice(g * 8, (g + 1) * 8)
            d_scr[:, place, :] = d.reshape(tok // 8, 8, LANES)
            dx = d * act_scr[at, :, cols].astype(jnp.float32)
            x_scr[:, place, :] = dx.reshape(tok // 8, 8, LANES)
        for n in range(states):
            row = (VECTORS + n) * ROWS
            a_scr[n] = jnp.exp(par_scr[at, row : row + ROWS, :]) * (-LOG2E)

        def block(i, carry):
            hs, cum = carry
            hs = list(hs)
            for o in range(16):
                t = i * 16 + o
                tile = i * 2 + o // 8
                d = d_scr[tile, pl.ds(o % 8, ROWS, stride=8), :]
                dx = x_scr[tile, pl.ds(o % 8, ROWS, stride=8), :]
                cum = cum + d
                acc = [None] * 4
                for n in range(states):
                    b = b_scr[pl.ds(n * tok + t, ROWS, stride=0), :]
                    c = c_ref[pl.ds(n * tok + t, ROWS, stride=0), :]
                    hs[n] = jnp.exp2(a_scr[n] * d) * hs[n] + dx * b
                    term = c * hs[n]
                    acc[n % 4] = term if acc[n % 4] is None else acc[n % 4] + term
                y_ref[t] = (acc[0] + acc[1]) + (acc[2] + acc[3])
                cum_ref[t] = cum
            return tuple(hs), cum

        zero = jnp.zeros((ROWS, LANES), jnp.float32)
        hs, cum = lax.fori_loop(0, tok // 16, block, ((zero,) * states, zero))
        for q in range(ROWS // 2):
            pair = slice(2 * q, 2 * q + 2)
            for n in range(states):
                end_ref[q, 2 * n : 2 * n + 2, :] = hs[n][pair]
            for k in range(4):
                row = 2 * states + 2 * k
                end_ref[q, row : row + 2, :] = cum[pair]


def scan_pass(info, x, rim, pieces, rank, states, count):
    tok, chans = x.shape
    rows, cols = pieces[0].shape[4:]
    many = chans // WIDE
    groups = chans // LANES
    sent = 2 * states + 8

    def turn(shape, where):
        def index(i, s):
            later = jnp.maximum(i - many, 0)
            return (0,) * where + (later,) + (0,) * (len(shape) - 1 - where)

        return pl.BlockSpec(shape, index)

    return pl.pallas_call(
        scan_kernel,
        grid_spec=pltpu.PrefetchScalarGridSpec(
            num_scalar_prefetch=1,
            grid=(2 * many,),
            in_specs=[
                pl.BlockSpec((tok, WIDE), lambda i, s: (0, jnp.minimum(i, many - 1))),
                pl.BlockSpec((8, WIDE), lambda i, s: (0, jnp.minimum(i, many - 1))),
                *piece_specs(pieces),
            ],
            out_specs=[
                pl.BlockSpec((tok, WIDE), lambda i, s: (0, jnp.minimum(i, many - 1))),
                pl.BlockSpec((count, ROWS, LANES), lambda i, s: (0, jnp.minimum(i, many - 1), 0)),
                turn((tok, ROWS, LANES), 1),
                turn((tok, ROWS, LANES), 1),
                turn((ROWS // 2, sent, LANES), 0),
                whole((tok * states, LANES)),
            ],
            scratch_shapes=[
                pltpu.VMEM((tok, cols - rank), jnp.float32),
                pltpu.VMEM((tok, rank), jnp.bfloat16),
                pltpu.VMEM((tok * states, LANES), jnp.float32),
                pltpu.VMEM((many, tok, WIDE), jnp.bfloat16),
                pltpu.VMEM((many, count * ROWS, LANES), jnp.float32),
                pltpu.VMEM((2, tok + 8, LANES), jnp.float32),
                pltpu.VMEM((tok // 8, 8 * ROWS, LANES), jnp.float32),
                pltpu.VMEM((tok // 8, 8 * ROWS, LANES), jnp.float32),
                pltpu.VMEM((states, ROWS, LANES), jnp.float32),
                pltpu.VMEM((many, 4, 4, 2, 2 * rows, cols), jnp.bfloat16),
            ],
        ),
        out_shape=[
            jax.ShapeDtypeStruct((tok, chans), jnp.bfloat16),
            jax.ShapeDtypeStruct((count, groups, LANES), jnp.float32),
            jax.ShapeDtypeStruct((tok, groups, LANES), jnp.float32),
            jax.ShapeDtypeStruct((tok, groups, LANES), jnp.float32),
            jax.ShapeDtypeStruct((groups // 2, sent, LANES), jnp.float32),
            jax.ShapeDtypeStruct((tok * states, LANES), jnp.float32),
        ],
        compiler_params=settings(),
        name="scan_pass",
    )(info, x, rim, *pieces)


def prefix_kernel(end_ref, alog_ref, in_ref):
    blocks = end_ref.shape[0]
    rows = alog_ref.shape[0]
    a = [jnp.exp(alog_ref[r : r + 8, :]) * (-LOG2E) for r in range(0, rows, 8)]
    hs = [jnp.zeros((8, LANES), jnp.float32) for _ in a]
    for k in range(blocks):
        spent = end_ref[k, rows : rows + 8, :]
        for j in range(len(a)):
            in_ref[k, 8 * j : 8 * j + 8, :] = hs[j]
            hs[j] = jnp.exp2(a[j] * spent) * hs[j] + end_ref[k, 8 * j : 8 * j + 8, :]


def prefix(ends, alog):
    return pl.pallas_call(
        prefix_kernel,
        out_shape=jax.ShapeDtypeStruct((ends.shape[0], *alog.shape), jnp.float32),
        name="prefix",
    )(ends, alog)


def gate_kernel(len_ref, y_ref, cum_ref, hin_ref, par_ref, act_ref, z_ref, c_ref, out_ref, y_scr, a_scr, h_scr):
    tok = act_ref.shape[0]
    states = a_scr.shape[0]
    a_scr[...] = jnp.exp(par_ref[VECTORS : VECTORS + states]) * (-LOG2E)
    for q in range(ROWS // 2):
        for n in range(states):
            h_scr[n, 2 * q : 2 * q + 2, :] = hin_ref[q, 2 * n : 2 * n + 2, :]

    def block(i, carry):
        for o in range(8):
            t = i * 8 + o
            cum = cum_ref[t]
            acc = [y_ref[t]] + [None] * 3
            for n in range(states):
                c = c_ref[pl.ds(n * tok + t, ROWS, stride=0), :]
                term = (c * h_scr[n]) * jnp.exp2(a_scr[n] * cum)
                acc[n % 4] = term if acc[n % 4] is None else acc[n % 4] + term
            y_scr[i, pl.ds(o, ROWS, stride=8), :] = (acc[0] + acc[1]) + (acc[2] + acc[3])
        return carry

    lax.fori_loop(0, tok // 8, block, 0)
    keep = lax.broadcasted_iota(jnp.int32, (tok, LANES), 0) < len_ref[0]
    for g in range(ROWS):
        cols = slice(g * LANES, (g + 1) * LANES)
        y = y_scr[:, g * 8 : (g + 1) * 8, :].reshape(tok, LANES)
        z = z_ref[:, cols].astype(jnp.float32)
        out = (y + par_ref[6, g : g + 1, :] * act_ref[:, cols].astype(jnp.float32)) * (z * sigmoid(z))
        out_ref[:, cols] = jnp.where(keep, out, 0.0).astype(jnp.bfloat16)


def gate_pass(info, y, cum, hin, pars, act, z, c_wide):
    tok, chans = act.shape
    states = c_wide.shape[0] // tok
    columns = pl.BlockSpec((tok, WIDE), lambda i, *_: (0, i))
    return pl.pallas_call(
        gate_kernel,
        grid_spec=pltpu.PrefetchScalarGridSpec(
            num_scalar_prefetch=1,
            grid=(chans // WIDE,),
            in_specs=[
                per_step(tok),
                per_step(tok),
                pl.BlockSpec((ROWS // 2, 2 * states, LANES), lambda i, *_: (i, 0, 0)),
                per_step(pars.shape[0]),
                columns,
                columns,
                whole((tok * states, LANES)),
            ],
            out_specs=columns,
            scratch_shapes=[
                pltpu.VMEM((tok // 8, 8 * ROWS, LANES), jnp.float32),
                pltpu.VMEM((states, ROWS, LANES), jnp.float32),
                pltpu.VMEM((states, ROWS, LANES), jnp.float32),
            ],
        ),
        out_shape=jax.ShapeDtypeStruct((tok, chans), jnp.bfloat16),
        compiler_params=settings(),
        name="gate_pass",
    )(info, y, cum, hin, pars, act, z, c_wide)


def device(x, y, z, core):
    return ((z & 1) * 4 + y) * 32 + x * 8 + (z >> 1) * 2 + core


def fetch(value, move):
    route = []
    for x in range(4):
        for y in range(4):
            for z in range(8):
                for core in range(2):
                    route.append((device(*move(x, y, z, core)), device(x, y, z, core)))
    return lax.ppermute(value, ("group", "ctx"), route)


def onward(axis):
    def move(x, y, z, core):
        step = 1 - 2 * core
        return ((x + step) % 4, y, z, core) if axis == "x" else (x, (y + step) % 4, z, core)

    return move


def flip(axis, bit):
    def move(x, y, z, core):
        return x ^ (bit if axis == "x" else 0), y ^ (bit if axis == "y" else 0), z ^ (bit if axis == "z" else 0), core ^ (
            bit if axis == "core" else 0
        )

    return move


def double(value, axis, bit, own):
    other = fetch(value, flip(axis, bit))
    low = (own & bit) == 0
    return jnp.concatenate([jnp.where(low, value, other), jnp.where(low, other, value)], axis=0)


def farther(near, axis, own_core):
    return fetch(jnp.where(own_core == 0, near[:, :1], near[:, 1:]), onward(axis))


def swap(value):
    return fetch(value, flip("core", 1))


def row_of_four(value, axis, own_core):
    near = fetch(value, onward(axis))
    far = farther(near, axis, own_core)
    near_too, far_too = swap(near), swap(far)
    zero = own_core == 0
    far = jnp.concatenate([jnp.where(zero, far, far_too), jnp.where(zero, far_too, far)], axis=1)
    return jnp.concatenate([value, jnp.where(zero, near, near_too), far, jnp.where(zero, near_too, near)], axis=0)


def shards(
    hidden_x, gate_z, lengths, conv_weight, conv_bias, xproj_weight, dtproj_weight, dt_bias, a_log, skip_gain
):
    x, z = hidden_x[0], gate_z[0]
    tok, chans = x.shape
    taps = conv_weight.shape[0]
    rank = dtproj_weight.shape[0]
    states = a_log.shape[0]
    blocks = lax.axis_size("ctx")
    length = lengths[0]
    group, ctx = lax.axis_index("group"), lax.axis_index("ctx")
    own_x, own_y, own_core = ctx >> 3, group & 3, ctx & 1
    own_z = ((ctx >> 1) & 3) * 2 + (group >> 2)
    own = {"x": own_x, "y": own_y, "z": own_z, "core": own_core}
    info = jnp.stack([lengths[0, 0], own_x, own_y, own_core]).astype(jnp.int32)

    edge = jnp.arange(tok - (taps - 1), tok, dtype=jnp.int32)[:, None] < length
    edge = jnp.where(edge, x[tok - (taps - 1) :], jnp.bfloat16(0))
    rim = lax.ppermute(edge, "ctx", [(i, i + 1) for i in range(blocks - 1)])
    rim = jnp.concatenate([jnp.zeros((8 - (taps - 1), chans), x.dtype), rim], axis=0)

    small = jnp.concatenate([conv_weight, conv_bias[None], dt_bias[None], skip_gain[None], a_log, a_log[:1]], axis=0).T
    width, count = small.shape
    high = lax.reduce_precision(small, 8, 7)
    middle = lax.reduce_precision(small - high, 8, 7)
    last = (small - high) - middle
    parts = [v.astype(jnp.bfloat16) for v in (high, middle, last)]
    fill = -(xproj_weight.shape[1] + 3 * count + rank) % LANES
    parts += [jnp.zeros((width, fill), jnp.bfloat16), dtproj_weight.T]
    mats = jnp.concatenate([xproj_weight, *parts], axis=1)[None]
    for axis, bit in (("z", 1), ("z", 2), ("z", 4), ("core", 1)):
        mats = double(mats, axis, bit, own[axis])
    mats = mats.reshape(1, 2, 4, 2, *mats.shape[1:])
    upper = row_of_four(mats[..., : width // 2, :], "y", own_core)
    lower = row_of_four(mats[..., width // 2 :, :], "x", own_core)
    pieces = []
    for value, axis in ((upper, "x"), (lower, "y")):
        near = fetch(value, onward(axis))
        far = farther(near, axis, own_core)
        pieces += [value, near, swap(near), far, swap(far)]

    act, pars, y, cum, ends, c_wide = scan_pass(info, x, rim, pieces, rank, states, count)
    mine = lax.dynamic_slice_in_dim(pars[VECTORS : VECTORS + states], 2 * ctx, 2, axis=1).reshape(2 * states, LANES)
    ends = lax.all_to_all(ends, "ctx", split_axis=0, concat_axis=0, tiled=True)
    hin = prefix(ends, mine)
    hin = lax.all_to_all(hin, "ctx", split_axis=0, concat_axis=0, tiled=True)
    out = gate_pass(info, y, cum, hin, pars, act, z, c_wide)
    return out[None]


def solution(mesh):
    spread = ("group", "ctx")
    in_specs = (
        P("group", "ctx", None),
        P("group", "ctx", None),
        P("group", "ctx"),
        P(None, spread),
        P(spread),
        P(spread, None),
        P(None, spread),
        P(spread),
        P(None, spread),
        P(spread),
    )
    return jax.shard_map(
        shards, mesh=mesh, in_specs=in_specs, out_specs=P("group", "ctx", None), check_vma=False
    )
```

```python
import jax
import jax.numpy as jnp
from jax import lax
from jax.experimental import pallas as pl
from jax.experimental.pallas import tpu as pltpu
from jax.sharding import PartitionSpec as P

LOG2E = 1.4426950408889634
LANES = 128
ROWS = 8
VECTORS = 7
WIDE = ROWS * LANES


def sigmoid(v):
    return 1.0 / (1.0 + jnp.exp(-v))


def log_one_plus(u):
    w = 1.0 + u
    return jnp.log(w) + (u - (w - 1.0))


def settings():
    return pltpu.CompilerParams(dimension_semantics=("arbitrary",), vmem_limit_bytes=56 << 20)


def whole(shape):
    return pl.BlockSpec(shape, lambda i, *_: (0,) * len(shape))


def per_step(count):
    return pl.BlockSpec((count, ROWS, LANES), lambda i, *_: (0, i, 0))


def piece_specs(pieces):
    specs = []
    for k, p in enumerate(pieces):
        rest = (p.shape[1], p.shape[2], 1, *p.shape[4:])
        if k < len(pieces) // 2:
            specs.append(
                pl.BlockSpec((1, *rest), lambda i, s: ((jnp.minimum(i, 7) - s[2]) & 3, 0, 0, jnp.minimum(i, 7) // 4, 0, 0))
            )
        else:
            specs.append(pl.BlockSpec((4, *rest), lambda i, s: (0, 0, 0, jnp.minimum(i, 7) // 4, 0, 0)))
    return specs


def assemble(step, info_ref, piece_refs, w_ref):
    own_x, own_y, own_core = info_ref[1], info_ref[2], info_ref[3]
    half = piece_refs[0].shape[4]
    many = len(piece_refs) // 2
    ahead = 1 + 2 * own_core
    away = (0, ahead, 4 - ahead, 2, 2)
    first = (0, 0, 0, own_core, 1 - own_core)
    for j, ref in enumerate(piece_refs[:many]):
        at = (own_x + away[j]) & 3
        for core in range(ref.shape[1]):
            for h in range(ref.shape[2]):
                w_ref[at, h, first[j] + core, 0:half, :] = ref[0, core, h, 0]
    wanted = (step - own_y) & 3
    for j, ref in enumerate(piece_refs[many:]):

        @pl.when(wanted == away[j])
        def _(ref=ref, first=first[j]):
            for q in range(4):
                for core in range(ref.shape[1]):
                    for h in range(ref.shape[2]):
                        w_ref[(own_x + q) & 3, h, first + core, half : 2 * half, :] = ref[q, core, h, 0]


def scan_kernel(info_ref, x_ref, rim_ref, *refs):
    *piece_refs, act_ref, par_ref, y_ref, cum_ref, end_ref, c_ref = refs[:-10]
    sum_scr, low_scr, b_scr, act_scr, par_scr, pad_scr, d_scr, x_scr, a_scr, w_scr = refs[-10:]
    step = pl.program_id(0)
    many = act_scr.shape[0]
    tok, rank = low_scr.shape
    states = a_scr.shape[0]
    keep = lax.broadcasted_iota(jnp.int32, (tok, LANES), 0) < info_ref[0]

    @pl.when(step < many)
    def _():
        assemble(step, info_ref, piece_refs, w_scr.at[step])
        count = par_scr.shape[1] // ROWS
        after = rank + 2 * states
        for g in range(ROWS):
            cols = slice(g * LANES, (g + 1) * LANES)
            beside = w_scr[step, g // 2, 2 * (g % 2) : 2 * (g % 2) + 2].reshape(LANES, w_scr.shape[-1])
            beside = beside[:, after - after % LANES : after - after % LANES + LANES].astype(jnp.float32).T
            at = after % LANES
            parts = [beside[at + k * count : at + (k + 1) * count] for k in range(3)]
            vectors = (parts[0] + parts[1]) + parts[2]
            par_scr[step, pl.ds(g, count, stride=ROWS), :] = vectors
            par_ref[:, g, :] = vectors
            pad = jnp.concatenate(
                [rim_ref[:, cols].astype(jnp.float32), jnp.where(keep, x_ref[:, cols].astype(jnp.float32), 0.0)], axis=0
            )
            pad_scr[g % 2] = pad
            total = vectors[4:5] + vectors[0:1] * pad_scr[g % 2, 5 : 5 + tok, :]
            for k in range(1, 4):
                total = total + vectors[k : k + 1] * pad_scr[g % 2, 5 + k : 5 + k + tok, :]
            act = (total * sigmoid(total)).astype(jnp.bfloat16)
            act_ref[:, cols] = act
            act_scr[step, :, cols] = act
        weight = w_scr[step].reshape(WIDE, w_scr.shape[-1])[:, : sum_scr.shape[1]]
        part = jnp.dot(act_scr[step], weight, preferred_element_type=jnp.float32)

        @pl.when(step == 0)
        def _():
            sum_scr[...] = part

        @pl.when(step > 0)
        def _():
            sum_scr[...] += part

        @pl.when(step == many - 1)
        def _():
            low_scr[...] = sum_scr[:, :rank].astype(jnp.bfloat16)
            for n in range(states):
                for ref, col in ((b_scr, rank + n), (c_ref, rank + states + n)):
                    ref[n * tok : (n + 1) * tok, :] = jnp.broadcast_to(sum_scr[:, col : col + 1], (tok, LANES))

    @pl.when(step >= many)
    def _():
        at = step - many
        raw = lax.dot_general(
            low_scr[...],
            w_scr[at].reshape(WIDE, w_scr.shape[-1])[:, w_scr.shape[-1] - rank :],
            (((1,), (1,)), ((), ())),
            preferred_element_type=jnp.float32,
        )
        for g in range(ROWS):
            cols = slice(g * LANES, (g + 1) * LANES)
            v = raw[:, cols] + par_scr[at, 5 * ROWS + g : 5 * ROWS + g + 1, :]
            soft = jnp.maximum(v, 0.0) + log_one_plus(jnp.exp(-jnp.abs(v)))
            d = jnp.where(keep, soft, 0.0)
            place = slice(g * 8, (g + 1) * 8)
            d_scr[:, place, :] = d.reshape(tok // 8, 8, LANES)
            dx = d * act_scr[at, :, cols].astype(jnp.float32)
            x_scr[:, place, :] = dx.reshape(tok // 8, 8, LANES)
        for n in range(states):
            row = (VECTORS + n) * ROWS
            a_scr[n] = jnp.exp(par_scr[at, row : row + ROWS, :]) * (-LOG2E)

        def block(i, carry):
            hs, cum = carry
            hs = list(hs)
            for o in range(16):
                t = i * 16 + o
                tile = i * 2 + o // 8
                d = d_scr[tile, pl.ds(o % 8, ROWS, stride=8), :]
                dx = x_scr[tile, pl.ds(o % 8, ROWS, stride=8), :]
                cum = cum + d
                acc = [None] * 4
                for n in range(states):
                    b = b_scr[pl.ds(n * tok + t, ROWS, stride=0), :]
                    c = c_ref[pl.ds(n * tok + t, ROWS, stride=0), :]
                    hs[n] = jnp.exp2(a_scr[n] * d) * hs[n] + dx * b
                    term = c * hs[n]
                    acc[n % 4] = term if acc[n % 4] is None else acc[n % 4] + term
                y_ref[t] = (acc[0] + acc[1]) + (acc[2] + acc[3])
                cum_ref[t] = cum
            return tuple(hs), cum

        zero = jnp.zeros((ROWS, LANES), jnp.float32)
        hs, cum = lax.fori_loop(0, tok // 16, block, ((zero,) * states, zero))
        for q in range(ROWS // 2):
            pair = slice(2 * q, 2 * q + 2)
            for n in range(states):
                end_ref[q, 2 * n : 2 * n + 2, :] = hs[n][pair]
            for k in range(4):
                row = 2 * states + 2 * k
                end_ref[q, row : row + 2, :] = cum[pair]


def scan_pass(info, x, rim, pieces, rank, states, count):
    tok, chans = x.shape
    rows, cols = pieces[0].shape[4:]
    many = chans // WIDE
    groups = chans // LANES
    sent = 2 * states + 8

    def turn(shape, where):
        def index(i, s):
            later = jnp.maximum(i - many, 0)
            return (0,) * where + (later,) + (0,) * (len(shape) - 1 - where)

        return pl.BlockSpec(shape, index)

    return pl.pallas_call(
        scan_kernel,
        grid_spec=pltpu.PrefetchScalarGridSpec(
            num_scalar_prefetch=1,
            grid=(2 * many,),
            in_specs=[
                pl.BlockSpec((tok, WIDE), lambda i, s: (0, jnp.minimum(i, many - 1))),
                pl.BlockSpec((8, WIDE), lambda i, s: (0, jnp.minimum(i, many - 1))),
                *piece_specs(pieces),
            ],
            out_specs=[
                pl.BlockSpec((tok, WIDE), lambda i, s: (0, jnp.minimum(i, many - 1))),
                pl.BlockSpec((count, ROWS, LANES), lambda i, s: (0, jnp.minimum(i, many - 1), 0)),
                turn((tok, ROWS, LANES), 1),
                turn((tok, ROWS, LANES), 1),
                turn((ROWS // 2, sent, LANES), 0),
                whole((tok * states, LANES)),
            ],
            scratch_shapes=[
                pltpu.VMEM((tok, cols - rank), jnp.float32),
                pltpu.VMEM((tok, rank), jnp.bfloat16),
                pltpu.VMEM((tok * states, LANES), jnp.float32),
                pltpu.VMEM((many, tok, WIDE), jnp.bfloat16),
                pltpu.VMEM((many, count * ROWS, LANES), jnp.float32),
                pltpu.VMEM((2, tok + 8, LANES), jnp.float32),
                pltpu.VMEM((tok // 8, 8 * ROWS, LANES), jnp.float32),
                pltpu.VMEM((tok // 8, 8 * ROWS, LANES), jnp.float32),
                pltpu.VMEM((states, ROWS, LANES), jnp.float32),
                pltpu.VMEM((many, 4, 4, 2, 2 * rows, cols), jnp.bfloat16),
            ],
        ),
        out_shape=[
            jax.ShapeDtypeStruct((tok, chans), jnp.bfloat16),
            jax.ShapeDtypeStruct((count, groups, LANES), jnp.float32),
            jax.ShapeDtypeStruct((tok, groups, LANES), jnp.float32),
            jax.ShapeDtypeStruct((tok, groups, LANES), jnp.float32),
            jax.ShapeDtypeStruct((groups // 2, sent, LANES), jnp.float32),
            jax.ShapeDtypeStruct((tok * states, LANES), jnp.float32),
        ],
        compiler_params=settings(),
        name="scan_pass",
    )(info, x, rim, *pieces)


def combine_kernel(info_ref, ends_ref, other_ref, par_ref, out_ref, a_scr):
    pairs, sent, _ = out_ref.shape
    rows = sent - 8
    for p in range(pairs):
        for n in range(rows // 2):
            a_scr[p, 2 * n : 2 * n + 2, :] = par_ref[VECTORS + n, 2 * p : 2 * p + 2, :]
    earlier = info_ref[3] == 0
    for p in range(pairs):
        own, other = ends_ref[p], other_ref[p]
        head, tail = jnp.where(earlier, own, other), jnp.where(earlier, other, own)
        spent = tail[rows:]
        for r in range(0, rows, 8):
            decay = jnp.exp2(jnp.exp(a_scr[p, r : r + 8, :]) * (-LOG2E) * spent)
            out_ref[p, r : r + 8, :] = decay * head[r : r + 8] + tail[r : r + 8]
        out_ref[p, rows:, :] = head[rows:] + spent


def combine(info, ends, other, pars):
    pairs, sent, _ = ends.shape
    half = pl.BlockSpec((pairs // 2, sent, LANES), lambda i, s: (s[3], 0, 0))
    return pl.pallas_call(
        combine_kernel,
        grid_spec=pltpu.PrefetchScalarGridSpec(
            num_scalar_prefetch=1,
            grid=(1,),
            in_specs=[half, half, pl.BlockSpec((pars.shape[0], pairs, LANES), lambda i, s: (0, s[3], 0))],
            out_specs=whole((pairs // 2, sent, LANES)),
            scratch_shapes=[pltpu.VMEM((pairs // 2, sent - 8, LANES), jnp.float32)],
        ),
        out_shape=jax.ShapeDtypeStruct((pairs // 2, sent, LANES), jnp.float32),
        compiler_params=settings(),
        name="combine",
    )(info, ends, other, pars)


def prefix_kernel(end_ref, alog_ref, in_ref):
    blocks = end_ref.shape[0]
    rows = alog_ref.shape[0]
    a = [jnp.exp(alog_ref[r : r + 8, :]) * (-LOG2E) for r in range(0, rows, 8)]
    hs = [jnp.zeros((8, LANES), jnp.float32) for _ in a]
    for k in range(blocks):
        spent = end_ref[k, rows : rows + 8, :]
        for j in range(len(a)):
            in_ref[k, 8 * j : 8 * j + 8, :] = hs[j]
            hs[j] = jnp.exp2(a[j] * spent) * hs[j] + end_ref[k, 8 * j : 8 * j + 8, :]


def prefix(ends, alog):
    return pl.pallas_call(
        prefix_kernel,
        out_shape=jax.ShapeDtypeStruct((ends.shape[0], *alog.shape), jnp.float32),
        name="prefix",
    )(ends, alog)


def gate_kernel(
    info_ref, y_ref, cum_ref, hin_ref, hin_too_ref, other_ref, par_ref, act_ref, z_ref, c_ref, out_ref, y_scr, a_scr, h_scr, e_scr
):
    tok = act_ref.shape[0]
    states = a_scr.shape[0]
    a_scr[...] = jnp.exp(par_ref[VECTORS : VECTORS + states]) * (-LOG2E)
    core = info_ref[3]
    own_half = pl.program_id(0) // 4 == core

    @pl.when(own_half)
    def _():
        for q in range(ROWS // 2):
            for n in range(states):
                h_scr[n, 2 * q : 2 * q + 2, :] = hin_ref[q, 2 * n : 2 * n + 2, :]

    @pl.when(jnp.logical_not(own_half))
    def _():
        for q in range(ROWS // 2):
            for n in range(states):
                h_scr[n, 2 * q : 2 * q + 2, :] = hin_too_ref[q, 2 * n : 2 * n + 2, :]

    @pl.when(core == 1)
    def _():
        for q in range(ROWS // 2):
            for n in range(states + 1):
                e_scr[n, 2 * q : 2 * q + 2, :] = other_ref[q, 2 * n : 2 * n + 2, :]
        for n in range(states):
            h_scr[n] = jnp.exp2(a_scr[n] * e_scr[states]) * h_scr[n] + e_scr[n]

    def block(i, carry):
        for o in range(8):
            t = i * 8 + o
            cum = cum_ref[t]
            acc = [y_ref[t]] + [None] * 3
            for n in range(states):
                c = c_ref[pl.ds(n * tok + t, ROWS, stride=0), :]
                term = (c * h_scr[n]) * jnp.exp2(a_scr[n] * cum)
                acc[n % 4] = term if acc[n % 4] is None else acc[n % 4] + term
            y_scr[i, pl.ds(o, ROWS, stride=8), :] = (acc[0] + acc[1]) + (acc[2] + acc[3])
        return carry

    lax.fori_loop(0, tok // 8, block, 0)
    keep = lax.broadcasted_iota(jnp.int32, (tok, LANES), 0) < info_ref[0]
    for g in range(ROWS):
        cols = slice(g * LANES, (g + 1) * LANES)
        y = y_scr[:, g * 8 : (g + 1) * 8, :].reshape(tok, LANES)
        z = z_ref[:, cols].astype(jnp.float32)
        out = (y + par_ref[6, g : g + 1, :] * act_ref[:, cols].astype(jnp.float32)) * (z * sigmoid(z))
        out_ref[:, cols] = jnp.where(keep, out, 0.0).astype(jnp.bfloat16)


def gate_pass(info, y, cum, hin, hin_too, other, pars, act, z, c_wide):
    tok, chans = act.shape
    states = c_wide.shape[0] // tok
    columns = pl.BlockSpec((tok, WIDE), lambda i, *_: (0, i))
    return pl.pallas_call(
        gate_kernel,
        grid_spec=pltpu.PrefetchScalarGridSpec(
            num_scalar_prefetch=1,
            grid=(chans // WIDE,),
            in_specs=[
                per_step(tok),
                per_step(tok),
                pl.BlockSpec((ROWS // 2, 2 * states, LANES), lambda i, *_: (i % 4, 0, 0)),
                pl.BlockSpec((ROWS // 2, 2 * states, LANES), lambda i, *_: (i % 4, 0, 0)),
                pl.BlockSpec((ROWS // 2, other.shape[1], LANES), lambda i, *_: (i, 0, 0)),
                per_step(pars.shape[0]),
                columns,
                columns,
                whole((tok * states, LANES)),
            ],
            out_specs=columns,
            scratch_shapes=[
                pltpu.VMEM((tok // 8, 8 * ROWS, LANES), jnp.float32),
                pltpu.VMEM((states, ROWS, LANES), jnp.float32),
                pltpu.VMEM((states, ROWS, LANES), jnp.float32),
                pltpu.VMEM((states + 1, ROWS, LANES), jnp.float32),
            ],
        ),
        out_shape=jax.ShapeDtypeStruct((tok, chans), jnp.bfloat16),
        compiler_params=settings(),
        name="gate_pass",
    )(info, y, cum, hin, hin_too, other, pars, act, z, c_wide)


def device(x, y, z, core):
    return ((z & 1) * 4 + y) * 32 + x * 8 + (z >> 1) * 2 + core


def fetch(value, move):
    route = []
    for x in range(4):
        for y in range(4):
            for z in range(8):
                for core in range(2):
                    route.append((device(*move(x, y, z, core)), device(x, y, z, core)))
    return lax.ppermute(value, ("group", "ctx"), route)


def onward(axis):
    def move(x, y, z, core):
        step = 1 - 2 * core
        return ((x + step) % 4, y, z, core) if axis == "x" else (x, (y + step) % 4, z, core)

    return move


def flip(axis, bit):
    def move(x, y, z, core):
        return x ^ (bit if axis == "x" else 0), y ^ (bit if axis == "y" else 0), z ^ (bit if axis == "z" else 0), core ^ (
            bit if axis == "core" else 0
        )

    return move


def double(value, axis, bit, own):
    other = fetch(value, flip(axis, bit))
    low = (own & bit) == 0
    return jnp.concatenate([jnp.where(low, value, other), jnp.where(low, other, value)], axis=0)


def farther(near, axis, own_core):
    return fetch(jnp.where(own_core == 0, near[:, :1], near[:, 1:]), onward(axis))


def swap(value):
    return fetch(value, flip("core", 1))


def row_of_four(value, axis, own_core):
    near = fetch(value, onward(axis))
    far = farther(near, axis, own_core)
    near_too, far_too = swap(near), swap(far)
    zero = own_core == 0
    far = jnp.concatenate([jnp.where(zero, far, far_too), jnp.where(zero, far_too, far)], axis=1)
    return jnp.concatenate([value, jnp.where(zero, near, near_too), far, jnp.where(zero, near_too, near)], axis=0)


def exchange(value):
    groups = [list(range(core, 32, 2)) for core in range(2)]
    return lax.all_to_all(value, "ctx", split_axis=0, concat_axis=0, tiled=True, axis_index_groups=groups)


def shards(
    hidden_x, gate_z, lengths, conv_weight, conv_bias, xproj_weight, dtproj_weight, dt_bias, a_log, skip_gain
):
    x, z = hidden_x[0], gate_z[0]
    tok, chans = x.shape
    taps = conv_weight.shape[0]
    rank = dtproj_weight.shape[0]
    states = a_log.shape[0]
    blocks = lax.axis_size("ctx")
    length = lengths[0]
    group, ctx = lax.axis_index("group"), lax.axis_index("ctx")
    own_x, own_y, own_core = ctx >> 3, group & 3, ctx & 1
    own_z = ((ctx >> 1) & 3) * 2 + (group >> 2)
    own = {"x": own_x, "y": own_y, "z": own_z, "core": own_core}
    info = jnp.stack([lengths[0, 0], own_x, own_y, own_core]).astype(jnp.int32)

    edge = jnp.arange(tok - (taps - 1), tok, dtype=jnp.int32)[:, None] < length
    edge = jnp.where(edge, x[tok - (taps - 1) :], jnp.bfloat16(0))
    rim = lax.ppermute(edge, "ctx", [(i, i + 1) for i in range(blocks - 1)])
    rim = jnp.concatenate([jnp.zeros((8 - (taps - 1), chans), x.dtype), rim], axis=0)

    small = jnp.concatenate([conv_weight, conv_bias[None], dt_bias[None], skip_gain[None], a_log, a_log[:1]], axis=0).T
    width, count = small.shape
    high = lax.reduce_precision(small, 8, 7)
    middle = lax.reduce_precision(small - high, 8, 7)
    last = (small - high) - middle
    parts = [v.astype(jnp.bfloat16) for v in (high, middle, last)]
    fill = -(xproj_weight.shape[1] + 3 * count + rank) % LANES
    parts += [jnp.zeros((width, fill), jnp.bfloat16), dtproj_weight.T]
    mats = jnp.concatenate([xproj_weight, *parts], axis=1)[None]
    mats, rim = lax.optimization_barrier((double(mats, "z", 1, own_z), rim))
    for axis, bit in (("z", 2), ("z", 4), ("core", 1)):
        mats = double(mats, axis, bit, own[axis])
    mats = mats.reshape(1, 2, 4, 2, *mats.shape[1:])
    upper = row_of_four(mats[..., : width // 2, :], "y", own_core)
    lower = row_of_four(mats[..., width // 2 :, :], "x", own_core)
    pieces = []
    for value, axis in ((upper, "x"), (lower, "y")):
        near = fetch(value, onward(axis))
        far = farther(near, axis, own_core)
        pieces += [value, near, swap(near), far, swap(far)]

    act, pars, y, cum, ends, c_wide = scan_pass(info, x, rim, pieces, rank, states, count)
    other = swap(ends)
    chip = combine(info, ends, other, pars)
    place = 2 * ((ctx & 1) * (blocks // 2) + (ctx >> 1))
    mine = lax.dynamic_slice_in_dim(pars[VECTORS : VECTORS + states], place, 2, axis=1).reshape(2 * states, LANES)
    chip = exchange(chip)
    hin = exchange(prefix(chip, mine))
    out = gate_pass(info, y, cum, hin, swap(hin), other, pars, act, z, c_wide)
    return out[None]


def solution(mesh):
    spread = ("group", "ctx")
    in_specs = (
        P("group", "ctx", None),
        P("group", "ctx", None),
        P("group", "ctx"),
        P(None, spread),
        P(spread),
        P(spread, None),
        P(None, spread),
        P(spread),
        P(None, spread),
        P(spread),
    )
    return jax.shard_map(
        shards, mesh=mesh, in_specs=in_specs, out_specs=P("group", "ctx", None), check_vma=False
    )
```

```python
import jax
import jax.numpy as jnp
from jax import lax
from jax.experimental import pallas as pl
from jax.experimental.pallas import tpu as pltpu
from jax.sharding import PartitionSpec as P

LOG2E = 1.4426950408889634
LANES = 128
ROWS = 8
VECTORS = 7
WIDE = ROWS * LANES


def sigmoid(v):
    return 1.0 / (1.0 + jnp.exp(-v))


def log_one_plus(u):
    w = 1.0 + u
    return jnp.log(w) + (u - (w - 1.0))


def settings():
    return pltpu.CompilerParams(dimension_semantics=("arbitrary",), vmem_limit_bytes=56 << 20)


def whole(shape):
    return pl.BlockSpec(shape, lambda i, *_: (0,) * len(shape))


def per_step(count):
    return pl.BlockSpec((count, ROWS, LANES), lambda i, *_: (0, i, 0))


def piece_specs(pieces):
    specs = []
    for k, p in enumerate(pieces):
        rest = (p.shape[1], 1, *p.shape[3:])
        if k < len(pieces) // 2:
            specs.append(
                pl.BlockSpec((1, *rest), lambda i, s: ((jnp.minimum(i, 7) - s[2]) & 3, 0, jnp.minimum(i, 7) // 4, 0, 0, 0))
            )
        else:
            specs.append(pl.BlockSpec((4, *rest), lambda i, s: (0, 0, jnp.minimum(i, 7) // 4, 0, 0, 0)))
    return specs


def assemble(step, info_ref, piece_refs, w_ref):
    own_x, own_y, own_core = info_ref[1], info_ref[2], info_ref[3]
    half = piece_refs[0].shape[4]
    many = len(piece_refs) // 2
    ahead = 1 + 2 * own_core
    away = (0, ahead, 4 - ahead, 2, 2)
    first = (0, 0, 0, own_core, 1 - own_core)
    for j, ref in enumerate(piece_refs[:many]):
        at = (own_x + away[j]) & 3
        for core in range(ref.shape[1]):
            for h in range(4):
                w_ref[at, (0, 2, 1, 3)[h], first[j] + core, 0:half, :] = ref[0, core, 0, h]
    wanted = (step - own_y) & 3
    for j, ref in enumerate(piece_refs[many:]):

        @pl.when(wanted == away[j])
        def _(ref=ref, first=first[j]):
            for q in range(4):
                for core in range(ref.shape[1]):
                    for h in range(4):
                        w_ref[(own_x + q) & 3, (0, 2, 1, 3)[h], first + core, half : 2 * half, :] = ref[q, core, 0, h]


def scan_kernel(info_ref, x_ref, rim_ref, *refs):
    *piece_refs, act_ref, par_ref, y_ref, cum_ref, end_ref, c_ref = refs[:-10]
    sum_scr, low_scr, b_scr, act_scr, par_scr, pad_scr, d_scr, x_scr, a_scr, w_scr = refs[-10:]
    step = pl.program_id(0)
    many = act_scr.shape[0]
    tok, rank = low_scr.shape
    states = a_scr.shape[0]
    keep = lax.broadcasted_iota(jnp.int32, (tok, LANES), 0) < info_ref[0]

    @pl.when(step < many)
    def _():
        assemble(step, info_ref, piece_refs, w_scr.at[step])
        count = par_scr.shape[1] // ROWS
        after = rank + 2 * states
        for g in range(ROWS):
            cols = slice(g * LANES, (g + 1) * LANES)
            beside = w_scr[step, g // 2, 2 * (g % 2) : 2 * (g % 2) + 2].reshape(LANES, w_scr.shape[-1])
            beside = beside[:, after - after % LANES : after - after % LANES + LANES].astype(jnp.float32).T
            at = after % LANES
            parts = [beside[at + k * count : at + (k + 1) * count] for k in range(3)]
            vectors = (parts[0] + parts[1]) + parts[2]
            par_scr[step, pl.ds(g, count, stride=ROWS), :] = vectors
            par_ref[:, g, :] = vectors
            pad = jnp.concatenate(
                [rim_ref[:, cols].astype(jnp.float32), jnp.where(keep, x_ref[:, cols].astype(jnp.float32), 0.0)], axis=0
            )
            pad_scr[g % 2] = pad
            total = vectors[4:5] + vectors[0:1] * pad_scr[g % 2, 5 : 5 + tok, :]
            for k in range(1, 4):
                total = total + vectors[k : k + 1] * pad_scr[g % 2, 5 + k : 5 + k + tok, :]
            act = (total * sigmoid(total)).astype(jnp.bfloat16)
            act_ref[:, cols] = act
            act_scr[step, :, cols] = act
        weight = w_scr[step].reshape(WIDE, w_scr.shape[-1])[:, : sum_scr.shape[1]]
        part = jnp.dot(act_scr[step], weight, preferred_element_type=jnp.float32)

        @pl.when(step == 0)
        def _():
            sum_scr[...] = part

        @pl.when(step > 0)
        def _():
            sum_scr[...] += part

        @pl.when(step == many - 1)
        def _():
            low_scr[...] = sum_scr[:, :rank].astype(jnp.bfloat16)
            for n in range(states):
                for ref, col in ((b_scr, rank + n), (c_ref, rank + states + n)):
                    ref[n * tok : (n + 1) * tok, :] = jnp.broadcast_to(sum_scr[:, col : col + 1], (tok, LANES))

    @pl.when(step >= many)
    def _():
        at = step - many
        raw = lax.dot_general(
            low_scr[...],
            w_scr[at].reshape(WIDE, w_scr.shape[-1])[:, w_scr.shape[-1] - rank :],
            (((1,), (1,)), ((), ())),
            preferred_element_type=jnp.float32,
        )
        for g in range(ROWS):
            cols = slice(g * LANES, (g + 1) * LANES)
            v = raw[:, cols] + par_scr[at, 5 * ROWS + g : 5 * ROWS + g + 1, :]
            soft = jnp.maximum(v, 0.0) + log_one_plus(jnp.exp(-jnp.abs(v)))
            d = jnp.where(keep, soft, 0.0)
            place = slice(g * 8, (g + 1) * 8)
            d_scr[:, place, :] = d.reshape(tok // 8, 8, LANES)
            dx = d * act_scr[at, :, cols].astype(jnp.float32)
            x_scr[:, place, :] = dx.reshape(tok // 8, 8, LANES)
        for n in range(states):
            row = (VECTORS + n) * ROWS
            a_scr[n] = jnp.exp(par_scr[at, row : row + ROWS, :]) * (-LOG2E)

        def block(i, carry):
            hs, cum = carry
            hs = list(hs)
            for o in range(16):
                t = i * 16 + o
                tile = i * 2 + o // 8
                d = d_scr[tile, pl.ds(o % 8, ROWS, stride=8), :]
                dx = x_scr[tile, pl.ds(o % 8, ROWS, stride=8), :]
                cum = cum + d
                acc = [None] * 4
                for n in range(states):
                    b = b_scr[pl.ds(n * tok + t, ROWS, stride=0), :]
                    c = c_ref[pl.ds(n * tok + t, ROWS, stride=0), :]
                    hs[n] = jnp.exp2(a_scr[n] * d) * hs[n] + dx * b
                    term = c * hs[n]
                    acc[n % 4] = term if acc[n % 4] is None else acc[n % 4] + term
                y_ref[t] = (acc[0] + acc[1]) + (acc[2] + acc[3])
                cum_ref[t] = cum
            return tuple(hs), cum

        zero = jnp.zeros((ROWS, LANES), jnp.float32)
        hs, cum = lax.fori_loop(0, tok // 16, block, ((zero,) * states, zero))
        for q in range(ROWS // 2):
            pair = slice(2 * q, 2 * q + 2)
            for n in range(states):
                end_ref[q, 2 * n : 2 * n + 2, :] = hs[n][pair]
            for k in range(4):
                row = 2 * states + 2 * k
                end_ref[q, row : row + 2, :] = cum[pair]


def scan_pass(info, x, rim, pieces, rank, states, count):
    tok, chans = x.shape
    rows, cols = pieces[0].shape[4:]
    many = chans // WIDE
    groups = chans // LANES
    sent = 2 * states + 8

    def turn(shape, where):
        def index(i, s):
            later = jnp.maximum(i - many, 0)
            return (0,) * where + (later,) + (0,) * (len(shape) - 1 - where)

        return pl.BlockSpec(shape, index)

    return pl.pallas_call(
        scan_kernel,
        grid_spec=pltpu.PrefetchScalarGridSpec(
            num_scalar_prefetch=1,
            grid=(2 * many,),
            in_specs=[
                pl.BlockSpec((tok, WIDE), lambda i, s: (0, jnp.minimum(i, many - 1))),
                pl.BlockSpec((8, WIDE), lambda i, s: (0, jnp.minimum(i, many - 1))),
                *piece_specs(pieces),
            ],
            out_specs=[
                pl.BlockSpec((tok, WIDE), lambda i, s: (0, jnp.minimum(i, many - 1))),
                pl.BlockSpec((count, ROWS, LANES), lambda i, s: (0, jnp.minimum(i, many - 1), 0)),
                turn((tok, ROWS, LANES), 1),
                turn((tok, ROWS, LANES), 1),
                turn((ROWS // 2, sent, LANES), 0),
                whole((tok * states, LANES)),
            ],
            scratch_shapes=[
                pltpu.VMEM((tok, cols - rank), jnp.float32),
                pltpu.VMEM((tok, rank), jnp.bfloat16),
                pltpu.VMEM((tok * states, LANES), jnp.float32),
                pltpu.VMEM((many, tok, WIDE), jnp.bfloat16),
                pltpu.VMEM((many, count * ROWS, LANES), jnp.float32),
                pltpu.VMEM((2, tok + 8, LANES), jnp.float32),
                pltpu.VMEM((tok // 8, 8 * ROWS, LANES), jnp.float32),
                pltpu.VMEM((tok // 8, 8 * ROWS, LANES), jnp.float32),
                pltpu.VMEM((states, ROWS, LANES), jnp.float32),
                pltpu.VMEM((many, 4, 4, 2, 2 * rows, cols), jnp.bfloat16),
            ],
        ),
        out_shape=[
            jax.ShapeDtypeStruct((tok, chans), jnp.bfloat16),
            jax.ShapeDtypeStruct((count, groups, LANES), jnp.float32),
            jax.ShapeDtypeStruct((tok, groups, LANES), jnp.float32),
            jax.ShapeDtypeStruct((tok, groups, LANES), jnp.float32),
            jax.ShapeDtypeStruct((groups // 2, sent, LANES), jnp.float32),
            jax.ShapeDtypeStruct((tok * states, LANES), jnp.float32),
        ],
        compiler_params=settings(),
        name="scan_pass",
    )(info, x, rim, *pieces)


def combine_kernel(info_ref, ends_ref, other_ref, par_ref, out_ref, a_scr):
    pairs, sent, _ = out_ref.shape
    rows = sent - 8
    for p in range(pairs):
        for n in range(rows // 2):
            a_scr[p, 2 * n : 2 * n + 2, :] = par_ref[VECTORS + n, 2 * p : 2 * p + 2, :]
    earlier = info_ref[3] == 0
    for p in range(pairs):
        own, other = ends_ref[p], other_ref[p]
        head, tail = jnp.where(earlier, own, other), jnp.where(earlier, other, own)
        spent = tail[rows:]
        for r in range(0, rows, 8):
            decay = jnp.exp2(jnp.exp(a_scr[p, r : r + 8, :]) * (-LOG2E) * spent)
            out_ref[p, r : r + 8, :] = decay * head[r : r + 8] + tail[r : r + 8]
        out_ref[p, rows:, :] = head[rows:] + spent


def combine(info, ends, other, pars):
    pairs, sent, _ = ends.shape
    half = pl.BlockSpec((pairs // 2, sent, LANES), lambda i, s: (s[3], 0, 0))
    return pl.pallas_call(
        combine_kernel,
        grid_spec=pltpu.PrefetchScalarGridSpec(
            num_scalar_prefetch=1,
            grid=(1,),
            in_specs=[half, half, pl.BlockSpec((pars.shape[0], pairs, LANES), lambda i, s: (0, s[3], 0))],
            out_specs=whole((pairs // 2, sent, LANES)),
            scratch_shapes=[pltpu.VMEM((pairs // 2, sent - 8, LANES), jnp.float32)],
        ),
        out_shape=jax.ShapeDtypeStruct((pairs // 2, sent, LANES), jnp.float32),
        compiler_params=settings(),
        name="combine",
    )(info, ends, other, pars)


def prefix_kernel(end_ref, alog_ref, in_ref):
    blocks = end_ref.shape[0]
    rows = alog_ref.shape[0]
    a = [jnp.exp(alog_ref[r : r + 8, :]) * (-LOG2E) for r in range(0, rows, 8)]
    hs = [jnp.zeros((8, LANES), jnp.float32) for _ in a]
    for k in range(blocks):
        spent = end_ref[k, rows : rows + 8, :]
        for j in range(len(a)):
            in_ref[k, 8 * j : 8 * j + 8, :] = hs[j]
            hs[j] = jnp.exp2(a[j] * spent) * hs[j] + end_ref[k, 8 * j : 8 * j + 8, :]


def prefix(ends, alog):
    return pl.pallas_call(
        prefix_kernel,
        out_shape=jax.ShapeDtypeStruct((ends.shape[0], *alog.shape), jnp.float32),
        name="prefix",
    )(ends, alog)


def factor_kernel(info_ref, z_ref, out_ref):
    keep = lax.broadcasted_iota(jnp.int32, z_ref.shape, 0) < info_ref[0]
    z = z_ref[...].astype(jnp.float32)
    out_ref[...] = jnp.where(keep, z * sigmoid(z), 0.0)


def gate_factor(info, z):
    tok, chans = z.shape
    columns = pl.BlockSpec((tok, WIDE), lambda i, *_: (0, i))
    return pl.pallas_call(
        factor_kernel,
        grid_spec=pltpu.PrefetchScalarGridSpec(
            num_scalar_prefetch=1, grid=(chans // WIDE,), in_specs=[columns], out_specs=columns
        ),
        out_shape=jax.ShapeDtypeStruct((tok, chans), jnp.float32),
        compiler_params=settings(),
        name="gate_factor",
    )(info, z)


def gate_kernel(
    info_ref, y_ref, cum_ref, hin_ref, hin_too_ref, other_ref, par_ref, act_ref, factor_ref, c_ref, out_ref, y_scr, a_scr, h_scr, e_scr
):
    tok = act_ref.shape[0]
    states = a_scr.shape[0]
    a_scr[...] = jnp.exp(par_ref[VECTORS : VECTORS + states]) * (-LOG2E)
    core = info_ref[3]
    own_half = pl.program_id(0) // 4 == core

    @pl.when(own_half)
    def _():
        for q in range(ROWS // 2):
            for n in range(states):
                h_scr[n, 2 * q : 2 * q + 2, :] = hin_ref[q, 2 * n : 2 * n + 2, :]

    @pl.when(jnp.logical_not(own_half))
    def _():
        for q in range(ROWS // 2):
            for n in range(states):
                h_scr[n, 2 * q : 2 * q + 2, :] = hin_too_ref[q, 2 * n : 2 * n + 2, :]

    @pl.when(core == 1)
    def _():
        for q in range(ROWS // 2):
            for n in range(states + 1):
                e_scr[n, 2 * q : 2 * q + 2, :] = other_ref[q, 2 * n : 2 * n + 2, :]
        for n in range(states):
            h_scr[n] = jnp.exp2(a_scr[n] * e_scr[states]) * h_scr[n] + e_scr[n]

    def block(i, carry):
        for o in range(8):
            t = i * 8 + o
            cum = cum_ref[t]
            acc = [y_ref[t]] + [None] * 3
            for n in range(states):
                c = c_ref[pl.ds(n * tok + t, ROWS, stride=0), :]
                term = (c * h_scr[n]) * jnp.exp2(a_scr[n] * cum)
                acc[n % 4] = term if acc[n % 4] is None else acc[n % 4] + term
            y_scr[i, pl.ds(o, ROWS, stride=8), :] = (acc[0] + acc[1]) + (acc[2] + acc[3])
        return carry

    lax.fori_loop(0, tok // 8, block, 0)
    for g in range(ROWS):
        cols = slice(g * LANES, (g + 1) * LANES)
        y = y_scr[:, g * 8 : (g + 1) * 8, :].reshape(tok, LANES)
        direct = par_ref[6, g : g + 1, :] * act_ref[:, cols].astype(jnp.float32)
        out_ref[:, cols] = ((y + direct) * factor_ref[:, cols]).astype(jnp.bfloat16)


def gate_pass(info, y, cum, hin, hin_too, other, pars, act, factor, c_wide):
    tok, chans = act.shape
    states = c_wide.shape[0] // tok
    columns = pl.BlockSpec((tok, WIDE), lambda i, *_: (0, i))
    return pl.pallas_call(
        gate_kernel,
        grid_spec=pltpu.PrefetchScalarGridSpec(
            num_scalar_prefetch=1,
            grid=(chans // WIDE,),
            in_specs=[
                per_step(tok),
                per_step(tok),
                pl.BlockSpec((ROWS // 2, 2 * states, LANES), lambda i, *_: (i % 4, 0, 0)),
                pl.BlockSpec((ROWS // 2, 2 * states, LANES), lambda i, *_: (i % 4, 0, 0)),
                pl.BlockSpec((ROWS // 2, other.shape[1], LANES), lambda i, *_: (i, 0, 0)),
                per_step(pars.shape[0]),
                columns,
                columns,
                whole((tok * states, LANES)),
            ],
            out_specs=columns,
            scratch_shapes=[
                pltpu.VMEM((tok // 8, 8 * ROWS, LANES), jnp.float32),
                pltpu.VMEM((states, ROWS, LANES), jnp.float32),
                pltpu.VMEM((states, ROWS, LANES), jnp.float32),
                pltpu.VMEM((states + 1, ROWS, LANES), jnp.float32),
            ],
        ),
        out_shape=jax.ShapeDtypeStruct((tok, chans), jnp.bfloat16),
        compiler_params=settings(),
        name="gate_pass",
    )(info, y, cum, hin, hin_too, other, pars, act, factor, c_wide)


def device(x, y, z, core):
    return ((z & 1) * 4 + y) * 32 + x * 8 + (z >> 1) * 2 + core


def fetch(value, move):
    route = []
    for x in range(4):
        for y in range(4):
            for z in range(8):
                for core in range(2):
                    route.append((device(*move(x, y, z, core)), device(x, y, z, core)))
    return lax.ppermute(value, ("group", "ctx"), route)


def onward(axis):
    def move(x, y, z, core):
        step = 1 - 2 * core
        return ((x + step) % 4, y, z, core) if axis == "x" else (x, (y + step) % 4, z, core)

    return move


def flip(axis, bit):
    def move(x, y, z, core):
        return x ^ (bit if axis == "x" else 0), y ^ (bit if axis == "y" else 0), z ^ (bit if axis == "z" else 0), core ^ (
            bit if axis == "core" else 0
        )

    return move


def double(value, axis, bit, own):
    other = fetch(value, flip(axis, bit))
    low = (own & bit) == 0
    return jnp.concatenate([jnp.where(low, value, other), jnp.where(low, other, value)], axis=0)


def farther(near, axis, own_core):
    return fetch(jnp.where(own_core == 0, near[:, :1], near[:, 1:]), onward(axis))


def swap(value):
    return fetch(value, flip("core", 1))


def row_of_four(value, axis, own_core):
    near = fetch(value, onward(axis))
    far = farther(near, axis, own_core)
    near_too, far_too = swap(near), swap(far)
    zero = own_core == 0
    far = jnp.concatenate([jnp.where(zero, far, far_too), jnp.where(zero, far_too, far)], axis=1)
    return jnp.concatenate([value, jnp.where(zero, near, near_too), far, jnp.where(zero, near_too, near)], axis=0)


def exchange(value):
    groups = [list(range(core, 32, 2)) for core in range(2)]
    return lax.all_to_all(value, "ctx", split_axis=0, concat_axis=0, tiled=True, axis_index_groups=groups)


def shards(
    hidden_x, gate_z, lengths, conv_weight, conv_bias, xproj_weight, dtproj_weight, dt_bias, a_log, skip_gain
):
    x, z = hidden_x[0], gate_z[0]
    tok, chans = x.shape
    taps = conv_weight.shape[0]
    rank = dtproj_weight.shape[0]
    states = a_log.shape[0]
    blocks = lax.axis_size("ctx")
    length = lengths[0]
    group, ctx = lax.axis_index("group"), lax.axis_index("ctx")
    own_x, own_y, own_core = ctx >> 3, group & 3, ctx & 1
    own_z = ((ctx >> 1) & 3) * 2 + (group >> 2)
    own = {"x": own_x, "y": own_y, "z": own_z, "core": own_core}
    info = jnp.stack([lengths[0, 0], own_x, own_y, own_core]).astype(jnp.int32)

    edge = jnp.arange(tok - (taps - 1), tok, dtype=jnp.int32)[:, None] < length
    edge = jnp.where(edge, x[tok - (taps - 1) :], jnp.bfloat16(0))
    rim = lax.ppermute(edge, "ctx", [(i, i + 1) for i in range(blocks - 1)])
    rim = jnp.concatenate([jnp.zeros((8 - (taps - 1), chans), x.dtype), rim], axis=0)

    small = jnp.concatenate([conv_weight, conv_bias[None], dt_bias[None], skip_gain[None], a_log, a_log[:1]], axis=0).T
    width, count = small.shape
    high = lax.reduce_precision(small, 8, 7)
    middle = lax.reduce_precision(small - high, 8, 7)
    last = (small - high) - middle
    parts = [v.astype(jnp.bfloat16) for v in (high, middle, last)]
    fill = -(xproj_weight.shape[1] + 3 * count + rank) % LANES
    parts += [jnp.zeros((width, fill), jnp.bfloat16), dtproj_weight.T]
    mats = jnp.concatenate([xproj_weight, *parts], axis=1)[None]
    mats, rim = lax.optimization_barrier((double(mats, "z", 4, own_z), rim))
    for axis, bit in (("z", 2), ("z", 1), ("core", 1)):
        mats = double(mats, axis, bit, own[axis])
    mats = mats.reshape(1, 2, 2, 4, *mats.shape[1:])
    upper = row_of_four(mats[..., : width // 2, :], "y", own_core)
    lower = row_of_four(mats[..., width // 2 :, :], "x", own_core)
    nears = fetch(upper, onward("x")), fetch(lower, onward("y"))
    *nears, factor = lax.optimization_barrier((*nears, gate_factor(info, z)))
    pieces = []
    for value, near, axis in ((upper, nears[0], "x"), (lower, nears[1], "y")):
        far = farther(near, axis, own_core)
        pieces += [value, near, swap(near), far, swap(far)]

    act, pars, y, cum, ends, c_wide = scan_pass(info, x, rim, pieces, rank, states, count)
    other = swap(ends)
    chip = combine(info, ends, other, pars)
    place = 2 * ((ctx & 1) * (blocks // 2) + (ctx >> 1))
    mine = lax.dynamic_slice_in_dim(pars[VECTORS : VECTORS + states], place, 2, axis=1).reshape(2 * states, LANES)
    chip = exchange(chip)
    hin = exchange(prefix(chip, mine))
    out = gate_pass(info, y, cum, hin, swap(hin), other, pars, act, factor, c_wide)
    return out[None]


def solution(mesh):
    spread = ("group", "ctx")
    in_specs = (
        P("group", "ctx", None),
        P("group", "ctx", None),
        P("group", "ctx"),
        P(None, spread),
        P(spread),
        P(spread, None),
        P(None, spread),
        P(spread),
        P(None, spread),
        P(spread),
    )
    return jax.shard_map(
        shards, mesh=mesh, in_specs=in_specs, out_specs=P("group", "ctx", None), check_vma=False
    )
```

```python
import jax
import jax.numpy as jnp
from jax import lax
from jax.experimental import pallas as pl
from jax.experimental.pallas import tpu as pltpu
from jax.sharding import PartitionSpec as P

LOG2E = 1.4426950408889634
LANES = 128
ROWS = 8
VECTORS = 7
WIDE = ROWS * LANES


def sigmoid(v):
    return 1.0 / (1.0 + jnp.exp(-v))


def log_one_plus(u):
    w = 1.0 + u
    return jnp.log(w) + (u - (w - 1.0))


def settings():
    return pltpu.CompilerParams(dimension_semantics=("arbitrary",), vmem_limit_bytes=56 << 20)


def whole(shape):
    return pl.BlockSpec(shape, lambda i, *_: (0,) * len(shape))


def per_step(count):
    return pl.BlockSpec((count, ROWS, LANES), lambda i, *_: (0, i, 0))


def piece_specs(pieces):
    specs = []
    for k, p in enumerate(pieces):
        rest = (p.shape[1], 1, *p.shape[3:])
        if k < len(pieces) // 2:
            specs.append(
                pl.BlockSpec((1, *rest), lambda i, s: ((jnp.minimum(i, 7) - s[2]) & 3, 0, jnp.minimum(i, 7) // 4, 0, 0, 0))
            )
        else:
            specs.append(pl.BlockSpec((4, *rest), lambda i, s: (0, 0, jnp.minimum(i, 7) // 4, 0, 0, 0)))
    return specs


def assemble(step, info_ref, piece_refs, w_ref):
    own_x, own_y, own_core = info_ref[1], info_ref[2], info_ref[3]
    half = piece_refs[0].shape[4]
    many = len(piece_refs) // 2
    ahead = 1 + 2 * own_core
    away = (0, ahead, 4 - ahead, 2, 2)
    first = (0, 0, 0, own_core, 1 - own_core)
    for j, ref in enumerate(piece_refs[:many]):
        at = (own_x + away[j]) & 3
        for core in range(ref.shape[1]):
            for h in range(4):
                w_ref[at, (0, 2, 1, 3)[h], first[j] + core, 0:half, :] = ref[0, core, 0, h]
    wanted = (step - own_y) & 3
    for j, ref in enumerate(piece_refs[many:]):

        @pl.when(wanted == away[j])
        def _(ref=ref, first=first[j]):
            for q in range(4):
                for core in range(ref.shape[1]):
                    for h in range(4):
                        w_ref[(own_x + q) & 3, (0, 2, 1, 3)[h], first + core, half : 2 * half, :] = ref[q, core, 0, h]


def scan_kernel(info_ref, x_ref, rim_ref, *refs):
    *piece_refs, act_ref, par_ref, y_ref, cum_ref, end_ref, c_ref = refs[:-10]
    sum_scr, low_scr, b_scr, act_scr, par_scr, pad_scr, d_scr, x_scr, a_scr, w_scr = refs[-10:]
    step = pl.program_id(0)
    many = act_scr.shape[0]
    tok, rank = low_scr.shape
    states = a_scr.shape[0]
    keep = lax.broadcasted_iota(jnp.int32, (tok, LANES), 0) < info_ref[0]

    @pl.when(step == 0)
    def _():
        sum_scr[...] = jnp.zeros_like(sum_scr)

    @pl.when(step < many)
    def _():
        assemble(step, info_ref, piece_refs, w_scr.at[step])
        acts = []
        count = par_scr.shape[1] // ROWS
        after = rank + 2 * states
        for g in range(ROWS):
            cols = slice(g * LANES, (g + 1) * LANES)
            beside = w_scr[step, g // 2, 2 * (g % 2) : 2 * (g % 2) + 2].reshape(LANES, w_scr.shape[-1])
            beside = beside[:, after - after % LANES : after - after % LANES + LANES].astype(jnp.float32).T
            at = after % LANES
            parts = [beside[at + k * count : at + (k + 1) * count] for k in range(3)]
            vectors = (parts[0] + parts[1]) + parts[2]
            par_scr[step, pl.ds(g, count, stride=ROWS), :] = vectors
            par_ref[:, g, :] = vectors
            pad = jnp.concatenate(
                [rim_ref[:, cols].astype(jnp.float32), jnp.where(keep, x_ref[:, cols].astype(jnp.float32), 0.0)], axis=0
            )
            pad_scr[g % 2] = pad
            total = vectors[4:5] + vectors[0:1] * pad_scr[g % 2, 5 : 5 + tok, :]
            for k in range(1, 4):
                total = total + vectors[k : k + 1] * pad_scr[g % 2, 5 + k : 5 + k + tok, :]
            act = (total * sigmoid(total)).astype(jnp.bfloat16)
            act_ref[:, cols] = act
            act_scr[step, :, cols] = act
            acts.append(act)
            if g % 2:
                weight = w_scr[step, g // 2].reshape(2 * LANES, w_scr.shape[-1])[:, : sum_scr.shape[1]]
                both = jnp.concatenate(acts[-2:], axis=1)
                sum_scr[...] += jnp.dot(both, weight, preferred_element_type=jnp.float32)
        @pl.when(step == many - 1)
        def _():
            low_scr[...] = sum_scr[:, :rank].astype(jnp.bfloat16)
            for n in range(states):
                for ref, col in ((b_scr, rank + n), (c_ref, rank + states + n)):
                    ref[n * tok : (n + 1) * tok, :] = jnp.broadcast_to(sum_scr[:, col : col + 1], (tok, LANES))

    @pl.when(step >= many)
    def _():
        at = step - many
        raw = lax.dot_general(
            low_scr[...],
            w_scr[at].reshape(WIDE, w_scr.shape[-1])[:, w_scr.shape[-1] - rank :],
            (((1,), (1,)), ((), ())),
            preferred_element_type=jnp.float32,
        )
        for g in range(ROWS):
            cols = slice(g * LANES, (g + 1) * LANES)
            v = raw[:, cols] + par_scr[at, 5 * ROWS + g : 5 * ROWS + g + 1, :]
            soft = jnp.maximum(v, 0.0) + log_one_plus(jnp.exp(-jnp.abs(v)))
            d = jnp.where(keep, soft, 0.0)
            place = slice(g * 8, (g + 1) * 8)
            d_scr[:, place, :] = d.reshape(tok // 8, 8, LANES)
            dx = d * act_scr[at, :, cols].astype(jnp.float32)
            x_scr[:, place, :] = dx.reshape(tok // 8, 8, LANES)
        for n in range(states):
            row = (VECTORS + n) * ROWS
            a_scr[n] = jnp.exp(par_scr[at, row : row + ROWS, :]) * (-LOG2E)

        def block(i, carry):
            hs, cum = carry
            hs = list(hs)
            for o in range(16):
                t = i * 16 + o
                tile = i * 2 + o // 8
                d = d_scr[tile, pl.ds(o % 8, ROWS, stride=8), :]
                dx = x_scr[tile, pl.ds(o % 8, ROWS, stride=8), :]
                cum = cum + d
                acc = [None] * 4
                for n in range(states):
                    b = b_scr[pl.ds(n * tok + t, ROWS, stride=0), :]
                    c = c_ref[pl.ds(n * tok + t, ROWS, stride=0), :]
                    hs[n] = jnp.exp2(a_scr[n] * d) * hs[n] + dx * b
                    term = c * hs[n]
                    acc[n % 4] = term if acc[n % 4] is None else acc[n % 4] + term
                y_ref[t] = (acc[0] + acc[1]) + (acc[2] + acc[3])
                cum_ref[t] = cum
            return tuple(hs), cum

        zero = jnp.zeros((ROWS, LANES), jnp.float32)
        hs, cum = lax.fori_loop(0, tok // 16, block, ((zero,) * states, zero))
        for q in range(ROWS // 2):
            pair = slice(2 * q, 2 * q + 2)
            for n in range(states):
                end_ref[q, 2 * n : 2 * n + 2, :] = hs[n][pair]
            for k in range(4):
                row = 2 * states + 2 * k
                end_ref[q, row : row + 2, :] = cum[pair]


def scan_pass(info, x, rim, pieces, rank, states, count):
    tok, chans = x.shape
    rows, cols = pieces[0].shape[4:]
    many = chans // WIDE
    groups = chans // LANES
    sent = 2 * states + 8

    def turn(shape, where):
        def index(i, s):
            later = jnp.maximum(i - many, 0)
            return (0,) * where + (later,) + (0,) * (len(shape) - 1 - where)

        return pl.BlockSpec(shape, index)

    return pl.pallas_call(
        scan_kernel,
        grid_spec=pltpu.PrefetchScalarGridSpec(
            num_scalar_prefetch=1,
            grid=(2 * many,),
            in_specs=[
                pl.BlockSpec((tok, WIDE), lambda i, s: (0, jnp.minimum(i, many - 1))),
                pl.BlockSpec((8, WIDE), lambda i, s: (0, jnp.minimum(i, many - 1))),
                *piece_specs(pieces),
            ],
            out_specs=[
                pl.BlockSpec((tok, WIDE), lambda i, s: (0, jnp.minimum(i, many - 1))),
                pl.BlockSpec((count, ROWS, LANES), lambda i, s: (0, jnp.minimum(i, many - 1), 0)),
                turn((tok, ROWS, LANES), 1),
                turn((tok, ROWS, LANES), 1),
                turn((ROWS // 2, sent, LANES), 0),
                whole((tok * states, LANES)),
            ],
            scratch_shapes=[
                pltpu.VMEM((tok, cols - rank), jnp.float32),
                pltpu.VMEM((tok, rank), jnp.bfloat16),
                pltpu.VMEM((tok * states, LANES), jnp.float32),
                pltpu.VMEM((many, tok, WIDE), jnp.bfloat16),
                pltpu.VMEM((many, count * ROWS, LANES), jnp.float32),
                pltpu.VMEM((2, tok + 8, LANES), jnp.float32),
                pltpu.VMEM((tok // 8, 8 * ROWS, LANES), jnp.float32),
                pltpu.VMEM((tok // 8, 8 * ROWS, LANES), jnp.float32),
                pltpu.VMEM((states, ROWS, LANES), jnp.float32),
                pltpu.VMEM((many, 4, 4, 2, 2 * rows, cols), jnp.bfloat16),
            ],
        ),
        out_shape=[
            jax.ShapeDtypeStruct((tok, chans), jnp.bfloat16),
            jax.ShapeDtypeStruct((count, groups, LANES), jnp.float32),
            jax.ShapeDtypeStruct((tok, groups, LANES), jnp.float32),
            jax.ShapeDtypeStruct((tok, groups, LANES), jnp.float32),
            jax.ShapeDtypeStruct((groups // 2, sent, LANES), jnp.float32),
            jax.ShapeDtypeStruct((tok * states, LANES), jnp.float32),
        ],
        compiler_params=settings(),
        name="scan_pass",
    )(info, x, rim, *pieces)


def combine_kernel(info_ref, ends_ref, other_ref, par_ref, out_ref, a_scr):
    pairs, sent, _ = out_ref.shape
    rows = sent - 8
    for p in range(pairs):
        for n in range(rows // 2):
            a_scr[p, 2 * n : 2 * n + 2, :] = par_ref[VECTORS + n, 2 * p : 2 * p + 2, :]
    earlier = info_ref[3] == 0
    for p in range(pairs):
        own, other = ends_ref[p], other_ref[p]
        head, tail = jnp.where(earlier, own, other), jnp.where(earlier, other, own)
        spent = tail[rows:]
        for r in range(0, rows, 8):
            decay = jnp.exp2(jnp.exp(a_scr[p, r : r + 8, :]) * (-LOG2E) * spent)
            out_ref[p, r : r + 8, :] = decay * head[r : r + 8] + tail[r : r + 8]
        out_ref[p, rows:, :] = head[rows:] + spent


def combine(info, ends, other, pars):
    pairs, sent, _ = ends.shape
    half = pl.BlockSpec((pairs // 2, sent, LANES), lambda i, s: (s[3], 0, 0))
    return pl.pallas_call(
        combine_kernel,
        grid_spec=pltpu.PrefetchScalarGridSpec(
            num_scalar_prefetch=1,
            grid=(1,),
            in_specs=[half, half, pl.BlockSpec((pars.shape[0], pairs, LANES), lambda i, s: (0, s[3], 0))],
            out_specs=whole((pairs // 2, sent, LANES)),
            scratch_shapes=[pltpu.VMEM((pairs // 2, sent - 8, LANES), jnp.float32)],
        ),
        out_shape=jax.ShapeDtypeStruct((pairs // 2, sent, LANES), jnp.float32),
        compiler_params=settings(),
        name="combine",
    )(info, ends, other, pars)


def prefix_kernel(end_ref, alog_ref, in_ref):
    blocks = end_ref.shape[0]
    rows = alog_ref.shape[0]
    a = [jnp.exp(alog_ref[r : r + 8, :]) * (-LOG2E) for r in range(0, rows, 8)]
    hs = [jnp.zeros((8, LANES), jnp.float32) for _ in a]
    for k in range(blocks):
        spent = end_ref[k, rows : rows + 8, :]
        for j in range(len(a)):
            in_ref[k, 8 * j : 8 * j + 8, :] = hs[j]
            hs[j] = jnp.exp2(a[j] * spent) * hs[j] + end_ref[k, 8 * j : 8 * j + 8, :]


def prefix(ends, alog):
    return pl.pallas_call(
        prefix_kernel,
        out_shape=jax.ShapeDtypeStruct((ends.shape[0], *alog.shape), jnp.float32),
        name="prefix",
    )(ends, alog)


def factor_kernel(info_ref, z_ref, out_ref):
    keep = lax.broadcasted_iota(jnp.int32, z_ref.shape, 0) < info_ref[0]
    z = z_ref[...].astype(jnp.float32)
    out_ref[...] = jnp.where(keep, z * sigmoid(z), 0.0)


def gate_factor(info, z):
    tok, chans = z.shape
    columns = pl.BlockSpec((tok, WIDE), lambda i, *_: (0, i))
    return pl.pallas_call(
        factor_kernel,
        grid_spec=pltpu.PrefetchScalarGridSpec(
            num_scalar_prefetch=1, grid=(chans // WIDE,), in_specs=[columns], out_specs=columns
        ),
        out_shape=jax.ShapeDtypeStruct((tok, chans), jnp.float32),
        compiler_params=settings(),
        name="gate_factor",
    )(info, z)


def gate_kernel(
    info_ref, y_ref, cum_ref, hin_ref, hin_too_ref, other_ref, par_ref, act_ref, factor_ref, c_ref, out_ref, y_scr, a_scr, h_scr, e_scr
):
    tok = act_ref.shape[0]
    states = a_scr.shape[0]
    a_scr[...] = jnp.exp(par_ref[VECTORS : VECTORS + states]) * (-LOG2E)
    core = info_ref[3]
    own_half = pl.program_id(0) // 4 == core

    @pl.when(own_half)
    def _():
        for q in range(ROWS // 2):
            for n in range(states):
                h_scr[n, 2 * q : 2 * q + 2, :] = hin_ref[q, 2 * n : 2 * n + 2, :]

    @pl.when(jnp.logical_not(own_half))
    def _():
        for q in range(ROWS // 2):
            for n in range(states):
                h_scr[n, 2 * q : 2 * q + 2, :] = hin_too_ref[q, 2 * n : 2 * n + 2, :]

    @pl.when(core == 1)
    def _():
        for q in range(ROWS // 2):
            for n in range(states + 1):
                e_scr[n, 2 * q : 2 * q + 2, :] = other_ref[q, 2 * n : 2 * n + 2, :]
        for n in range(states):
            h_scr[n] = jnp.exp2(a_scr[n] * e_scr[states]) * h_scr[n] + e_scr[n]

    def block(i, carry):
        for o in range(8):
            t = i * 8 + o
            cum = cum_ref[t]
            acc = [y_ref[t]] + [None] * 3
            for n in range(states):
                c = c_ref[pl.ds(n * tok + t, ROWS, stride=0), :]
                term = (c * h_scr[n]) * jnp.exp2(a_scr[n] * cum)
                acc[n % 4] = term if acc[n % 4] is None else acc[n % 4] + term
            y_scr[i, pl.ds(o, ROWS, stride=8), :] = (acc[0] + acc[1]) + (acc[2] + acc[3])
        return carry

    lax.fori_loop(0, tok // 8, block, 0)
    for g in range(ROWS):
        cols = slice(g * LANES, (g + 1) * LANES)
        y = y_scr[:, g * 8 : (g + 1) * 8, :].reshape(tok, LANES)
        direct = par_ref[6, g : g + 1, :] * act_ref[:, cols].astype(jnp.float32)
        out_ref[:, cols] = ((y + direct) * factor_ref[:, cols]).astype(jnp.bfloat16)


def gate_pass(info, y, cum, hin, hin_too, other, pars, act, factor, c_wide):
    tok, chans = act.shape
    states = c_wide.shape[0] // tok
    columns = pl.BlockSpec((tok, WIDE), lambda i, *_: (0, i))
    return pl.pallas_call(
        gate_kernel,
        grid_spec=pltpu.PrefetchScalarGridSpec(
            num_scalar_prefetch=1,
            grid=(chans // WIDE,),
            in_specs=[
                per_step(tok),
                per_step(tok),
                pl.BlockSpec((ROWS // 2, 2 * states, LANES), lambda i, *_: (i % 4, 0, 0)),
                pl.BlockSpec((ROWS // 2, 2 * states, LANES), lambda i, *_: (i % 4, 0, 0)),
                pl.BlockSpec((ROWS // 2, other.shape[1], LANES), lambda i, *_: (i, 0, 0)),
                per_step(pars.shape[0]),
                columns,
                columns,
                whole((tok * states, LANES)),
            ],
            out_specs=columns,
            scratch_shapes=[
                pltpu.VMEM((tok // 8, 8 * ROWS, LANES), jnp.float32),
                pltpu.VMEM((states, ROWS, LANES), jnp.float32),
                pltpu.VMEM((states, ROWS, LANES), jnp.float32),
                pltpu.VMEM((states + 1, ROWS, LANES), jnp.float32),
            ],
        ),
        out_shape=jax.ShapeDtypeStruct((tok, chans), jnp.bfloat16),
        compiler_params=settings(),
        name="gate_pass",
    )(info, y, cum, hin, hin_too, other, pars, act, factor, c_wide)


def device(x, y, z, core):
    return ((z & 1) * 4 + y) * 32 + x * 8 + (z >> 1) * 2 + core


def fetch(value, move):
    route = []
    for x in range(4):
        for y in range(4):
            for z in range(8):
                for core in range(2):
                    route.append((device(*move(x, y, z, core)), device(x, y, z, core)))
    return lax.ppermute(value, ("group", "ctx"), route)


def onward(axis):
    def move(x, y, z, core):
        step = 1 - 2 * core
        return ((x + step) % 4, y, z, core) if axis == "x" else (x, (y + step) % 4, z, core)

    return move


def flip(*bits):
    def move(x, y, z, core):
        z_bits = sum(bit for axis, bit in bits if axis == "z")
        core_bits = sum(bit for axis, bit in bits if axis == "core")
        return x, y, z ^ z_bits, core ^ core_bits

    return move


def four(value, low, high, own):
    at_low, at_high, at_both = fetch(value, flip(low)), fetch(value, flip(high)), fetch(value, flip(low, high))

    def pair(bit, here, there):
        zero = (own[bit[0]] & bit[1]) == 0
        return jnp.concatenate([jnp.where(zero, here, there), jnp.where(zero, there, here)], axis=0)

    return pair(high, pair(low, value, at_low), pair(low, at_high, at_both))


def farther(near, axis, own_core):
    return fetch(jnp.where(own_core == 0, near[:, :1], near[:, 1:]), onward(axis))


def swap(value):
    return fetch(value, flip(("core", 1)))


def row_of_four(value, axis, own_core):
    near = fetch(value, onward(axis))
    far = farther(near, axis, own_core)
    near_too, far_too = swap(near), swap(far)
    zero = own_core == 0
    far = jnp.concatenate([jnp.where(zero, far, far_too), jnp.where(zero, far_too, far)], axis=1)
    return jnp.concatenate([value, jnp.where(zero, near, near_too), far, jnp.where(zero, near_too, near)], axis=0)


def exchange(value):
    groups = [list(range(core, 32, 2)) for core in range(2)]
    return lax.all_to_all(value, "ctx", split_axis=0, concat_axis=0, tiled=True, axis_index_groups=groups)


def shards(
    hidden_x, gate_z, lengths, conv_weight, conv_bias, xproj_weight, dtproj_weight, dt_bias, a_log, skip_gain
):
    x, z = hidden_x[0], gate_z[0]
    tok, chans = x.shape
    taps = conv_weight.shape[0]
    rank = dtproj_weight.shape[0]
    states = a_log.shape[0]
    blocks = lax.axis_size("ctx")
    length = lengths[0]
    group, ctx = lax.axis_index("group"), lax.axis_index("ctx")
    own_x, own_y, own_core = ctx >> 3, group & 3, ctx & 1
    own_z = ((ctx >> 1) & 3) * 2 + (group >> 2)
    own = {"x": own_x, "y": own_y, "z": own_z, "core": own_core}
    info = jnp.stack([lengths[0, 0], own_x, own_y, own_core]).astype(jnp.int32)

    edge = jnp.arange(tok - (taps - 1), tok, dtype=jnp.int32)[:, None] < length
    edge = jnp.where(edge, x[tok - (taps - 1) :], jnp.bfloat16(0))
    rim = lax.ppermute(edge, "ctx", [(i, i + 1) for i in range(blocks - 1)])
    rim = jnp.concatenate([jnp.zeros((8 - (taps - 1), chans), x.dtype), rim], axis=0)

    small = jnp.concatenate([conv_weight, conv_bias[None], dt_bias[None], skip_gain[None], a_log, a_log[:1]], axis=0).T
    width, count = small.shape
    high = lax.reduce_precision(small, 8, 7)
    middle = lax.reduce_precision(small - high, 8, 7)
    last = (small - high) - middle
    parts = [v.astype(jnp.bfloat16) for v in (high, middle, last)]
    fill = -(xproj_weight.shape[1] + 3 * count + rank) % LANES
    parts += [jnp.zeros((width, fill), jnp.bfloat16), dtproj_weight.T]
    mats = jnp.concatenate([xproj_weight, *parts], axis=1)[None]
    mats, rim = lax.optimization_barrier((four(mats, ("z", 4), ("z", 2), own), rim))
    mats = four(mats, ("z", 1), ("core", 1), own)
    mats = mats.reshape(1, 2, 2, 4, *mats.shape[1:])
    upper = row_of_four(mats[..., : width // 2, :], "y", own_core)
    lower = row_of_four(mats[..., width // 2 :, :], "x", own_core)
    nears = fetch(upper, onward("x")), fetch(lower, onward("y"))
    *nears, factor = lax.optimization_barrier((*nears, gate_factor(info, z)))
    pieces = []
    for value, near, axis in ((upper, nears[0], "x"), (lower, nears[1], "y")):
        far = farther(near, axis, own_core)
        pieces += [value, near, swap(near), far, swap(far)]

    act, pars, y, cum, ends, c_wide = scan_pass(info, x, rim, pieces, rank, states, count)
    other = swap(ends)
    chip = combine(info, ends, other, pars)
    place = 2 * ((ctx & 1) * (blocks // 2) + (ctx >> 1))
    mine = lax.dynamic_slice_in_dim(pars[VECTORS : VECTORS + states], place, 2, axis=1).reshape(2 * states, LANES)
    chip = exchange(chip)
    hin = exchange(prefix(chip, mine))
    out = gate_pass(info, y, cum, hin, swap(hin), other, pars, act, factor, c_wide)
    return out[None]


def solution(mesh):
    spread = ("group", "ctx")
    in_specs = (
        P("group", "ctx", None),
        P("group", "ctx", None),
        P("group", "ctx"),
        P(None, spread),
        P(spread),
        P(spread, None),
        P(None, spread),
        P(spread),
        P(None, spread),
        P(spread),
    )
    return jax.shard_map(
        shards, mesh=mesh, in_specs=in_specs, out_specs=P("group", "ctx", None), check_vma=False
    )
```

```python
import jax
import jax.numpy as jnp
from jax import lax
from jax.experimental import pallas as pl
from jax.experimental.pallas import tpu as pltpu
from jax.sharding import PartitionSpec as P

LOG2E = 1.4426950408889634
LANES = 128
ROWS = 8
VECTORS = 7
WIDE = ROWS * LANES


def sigmoid(v):
    return 1.0 / (1.0 + jnp.exp(-v))


def log_one_plus(u):
    w = 1.0 + u
    return jnp.log(w) + (u - (w - 1.0))


def settings():
    return pltpu.CompilerParams(dimension_semantics=("arbitrary",), vmem_limit_bytes=56 << 20)


def whole(shape):
    return pl.BlockSpec(shape, lambda i, *_: (0,) * len(shape))


def per_step(count):
    return pl.BlockSpec((count, ROWS, LANES), lambda i, *_: (0, i, 0))


def piece_specs(pieces):
    specs = []
    for k, p in enumerate(pieces):
        rest = (p.shape[1], 1, *p.shape[3:])
        if k < len(pieces) // 2:
            specs.append(
                pl.BlockSpec((1, *rest), lambda i, s: ((jnp.minimum(i, 7) - s[2]) & 3, 0, jnp.minimum(i, 7) // 4, 0, 0, 0))
            )
        else:
            specs.append(pl.BlockSpec((4, *rest), lambda i, s: (0, 0, jnp.minimum(i, 7) // 4, 0, 0, 0)))
    return specs


def assemble(step, info_ref, piece_refs, w_ref):
    own_x, own_y, own_core = info_ref[1], info_ref[2], info_ref[3]
    half = piece_refs[0].shape[4]
    many = len(piece_refs) // 2
    ahead = 1 + 2 * own_core
    away = (0, ahead, 4 - ahead, 2, 2)
    first = (0, 0, 0, own_core, 1 - own_core)
    for j, ref in enumerate(piece_refs[:many]):
        at = (own_x + away[j]) & 3
        for core in range(ref.shape[1]):
            for h in range(4):
                w_ref[at, (0, 2, 1, 3)[h], first[j] + core, 0:half, :] = ref[0, core, 0, h]
    wanted = (step - own_y) & 3
    for j, ref in enumerate(piece_refs[many:]):

        @pl.when(wanted == away[j])
        def _(ref=ref, first=first[j]):
            for q in range(4):
                for core in range(ref.shape[1]):
                    for h in range(4):
                        w_ref[(own_x + q) & 3, (0, 2, 1, 3)[h], first + core, half : 2 * half, :] = ref[q, core, 0, h]


def scan_kernel(info_ref, x_ref, rim_ref, *refs):
    *piece_refs, act_ref, par_ref, y_ref, cum_ref, end_ref, c_ref = refs[:-10]
    sum_scr, low_scr, b_scr, act_scr, par_scr, pad_scr, d_scr, x_scr, a_scr, w_scr = refs[-10:]
    step = pl.program_id(0)
    many = act_scr.shape[0]
    tok, rank = low_scr.shape
    states = a_scr.shape[0]
    keep = lax.broadcasted_iota(jnp.int32, (tok, LANES), 0) < info_ref[0]

    @pl.when(step == 0)
    def _():
        sum_scr[...] = jnp.zeros_like(sum_scr)

    @pl.when(step < many)
    def _():
        assemble(step, info_ref, piece_refs, w_scr.at[step])
        acts = []
        count = par_scr.shape[1] // ROWS
        after = rank + 2 * states
        for g in range(ROWS):
            cols = slice(g * LANES, (g + 1) * LANES)
            beside = w_scr[step, g // 2, 2 * (g % 2) : 2 * (g % 2) + 2].reshape(LANES, w_scr.shape[-1])
            beside = beside[:, after - after % LANES : after - after % LANES + LANES].astype(jnp.float32).T
            at = after % LANES
            parts = [beside[at + k * count : at + (k + 1) * count] for k in range(3)]
            vectors = (parts[0] + parts[1]) + parts[2]
            par_scr[step, pl.ds(g, count, stride=ROWS), :] = vectors
            par_ref[:, g, :] = vectors
            pad = jnp.concatenate(
                [rim_ref[:, cols].astype(jnp.float32), jnp.where(keep, x_ref[:, cols].astype(jnp.float32), 0.0)], axis=0
            )
            pad_scr[g % 2] = pad
            total = vectors[4:5] + vectors[0:1] * pad_scr[g % 2, 5 : 5 + tok, :]
            for k in range(1, 4):
                total = total + vectors[k : k + 1] * pad_scr[g % 2, 5 + k : 5 + k + tok, :]
            act = (total * sigmoid(total)).astype(jnp.bfloat16)
            act_ref[:, cols] = act
            act_scr[step, :, cols] = act
            acts.append(act)
            if g % 2:
                weight = w_scr[step, g // 2].reshape(2 * LANES, w_scr.shape[-1])[:, : sum_scr.shape[1]]
                both = jnp.concatenate(acts[-2:], axis=1)
                sum_scr[...] += jnp.dot(both, weight, preferred_element_type=jnp.float32)
        @pl.when(step == many - 1)
        def _():
            low_scr[...] = sum_scr[:, :rank].astype(jnp.bfloat16)
            for n in range(states):
                for ref, col in ((b_scr, rank + n), (c_ref, rank + states + n)):
                    ref[n * tok : (n + 1) * tok, :] = jnp.broadcast_to(sum_scr[:, col : col + 1], (tok, LANES))

    @pl.when(step >= many)
    def _():
        at = step - many
        raw = lax.dot_general(
            low_scr[...],
            w_scr[at].reshape(WIDE, w_scr.shape[-1])[:, w_scr.shape[-1] - rank :],
            (((1,), (1,)), ((), ())),
            preferred_element_type=jnp.float32,
        )
        for g in range(ROWS):
            cols = slice(g * LANES, (g + 1) * LANES)
            v = raw[:, cols] + par_scr[at, 5 * ROWS + g : 5 * ROWS + g + 1, :]
            soft = jnp.maximum(v, 0.0) + log_one_plus(jnp.exp(-jnp.abs(v)))
            d = jnp.where(keep, soft, 0.0)
            place = slice(g * 8, (g + 1) * 8)
            d_scr[:, place, :] = d.reshape(tok // 8, 8, LANES)
            dx = d * act_scr[at, :, cols].astype(jnp.float32)
            x_scr[:, place, :] = dx.reshape(tok // 8, 8, LANES)
        for n in range(states):
            row = (VECTORS + n) * ROWS
            a_scr[n] = jnp.exp(par_scr[at, row : row + ROWS, :]) * (-LOG2E)

        def block(i, carry):
            hs, cum = carry
            hs = list(hs)
            for o in range(16):
                t = i * 16 + o
                tile = i * 2 + o // 8
                d = d_scr[tile, pl.ds(o % 8, ROWS, stride=8), :]
                dx = x_scr[tile, pl.ds(o % 8, ROWS, stride=8), :]
                cum = cum + d
                acc = [None] * 4
                for n in range(states):
                    b = b_scr[pl.ds(n * tok + t, ROWS, stride=0), :]
                    c = c_ref[pl.ds(n * tok + t, ROWS, stride=0), :]
                    hs[n] = jnp.exp2(a_scr[n] * d) * hs[n] + dx * b
                    term = c * hs[n]
                    acc[n % 4] = term if acc[n % 4] is None else acc[n % 4] + term
                y_ref[t] = (acc[0] + acc[1]) + (acc[2] + acc[3])
                cum_ref[t] = cum
            return tuple(hs), cum

        zero = jnp.zeros((ROWS, LANES), jnp.float32)
        hs, cum = lax.fori_loop(0, tok // 16, block, ((zero,) * states, zero))
        for q in range(ROWS // 2):
            pair = slice(2 * q, 2 * q + 2)
            for n in range(states):
                end_ref[q, 2 * n : 2 * n + 2, :] = hs[n][pair]
            for k in range(4):
                row = 2 * states + 2 * k
                end_ref[q, row : row + 2, :] = cum[pair]


def scan_pass(info, x, rim, pieces, rank, states, count):
    tok, chans = x.shape
    rows, cols = pieces[0].shape[4:]
    many = chans // WIDE
    groups = chans // LANES
    sent = 2 * states + 8

    def turn(shape, where):
        def index(i, s):
            later = jnp.maximum(i - many, 0)
            return (0,) * where + (later,) + (0,) * (len(shape) - 1 - where)

        return pl.BlockSpec(shape, index)

    return pl.pallas_call(
        scan_kernel,
        grid_spec=pltpu.PrefetchScalarGridSpec(
            num_scalar_prefetch=1,
            grid=(2 * many,),
            in_specs=[
                pl.BlockSpec((tok, WIDE), lambda i, s: (0, jnp.minimum(i, many - 1))),
                pl.BlockSpec((8, WIDE), lambda i, s: (0, jnp.minimum(i, many - 1))),
                *piece_specs(pieces),
            ],
            out_specs=[
                pl.BlockSpec((tok, WIDE), lambda i, s: (0, jnp.minimum(i, many - 1))),
                pl.BlockSpec((count, ROWS, LANES), lambda i, s: (0, jnp.minimum(i, many - 1), 0)),
                turn((tok, ROWS, LANES), 1),
                turn((tok, ROWS, LANES), 1),
                turn((ROWS // 2, sent, LANES), 0),
                whole((tok * states, LANES)),
            ],
            scratch_shapes=[
                pltpu.VMEM((tok, cols - rank), jnp.float32),
                pltpu.VMEM((tok, rank), jnp.bfloat16),
                pltpu.VMEM((tok * states, LANES), jnp.float32),
                pltpu.VMEM((many, tok, WIDE), jnp.bfloat16),
                pltpu.VMEM((many, count * ROWS, LANES), jnp.float32),
                pltpu.VMEM((2, tok + 8, LANES), jnp.float32),
                pltpu.VMEM((tok // 8, 8 * ROWS, LANES), jnp.float32),
                pltpu.VMEM((tok // 8, 8 * ROWS, LANES), jnp.float32),
                pltpu.VMEM((states, ROWS, LANES), jnp.float32),
                pltpu.VMEM((many, 4, 4, 2, 2 * rows, cols), jnp.bfloat16),
            ],
        ),
        out_shape=[
            jax.ShapeDtypeStruct((tok, chans), jnp.bfloat16),
            jax.ShapeDtypeStruct((count, groups, LANES), jnp.float32),
            jax.ShapeDtypeStruct((tok, groups, LANES), jnp.float32),
            jax.ShapeDtypeStruct((tok, groups, LANES), jnp.float32),
            jax.ShapeDtypeStruct((groups // 2, sent, LANES), jnp.float32),
            jax.ShapeDtypeStruct((tok * states, LANES), jnp.float32),
        ],
        compiler_params=settings(),
        name="scan_pass",
    )(info, x, rim, *pieces)


def combine_kernel(info_ref, ends_ref, other_ref, par_ref, out_ref, a_scr):
    pairs, sent, _ = out_ref.shape
    rows = sent - 8
    for p in range(pairs):
        for n in range(rows // 2):
            a_scr[p, 2 * n : 2 * n + 2, :] = par_ref[VECTORS + n, 2 * p : 2 * p + 2, :]
    earlier = info_ref[3] == 0
    for p in range(pairs):
        own, other = ends_ref[p], other_ref[p]
        head, tail = jnp.where(earlier, own, other), jnp.where(earlier, other, own)
        spent = tail[rows:]
        for r in range(0, rows, 8):
            decay = jnp.exp2(jnp.exp(a_scr[p, r : r + 8, :]) * (-LOG2E) * spent)
            out_ref[p, r : r + 8, :] = decay * head[r : r + 8] + tail[r : r + 8]
        out_ref[p, rows:, :] = head[rows:] + spent


def combine(info, ends, other, pars):
    pairs, sent, _ = ends.shape
    half = pl.BlockSpec((pairs // 2, sent, LANES), lambda i, s: (s[3], 0, 0))
    return pl.pallas_call(
        combine_kernel,
        grid_spec=pltpu.PrefetchScalarGridSpec(
            num_scalar_prefetch=1,
            grid=(1,),
            in_specs=[half, half, pl.BlockSpec((pars.shape[0], pairs, LANES), lambda i, s: (0, s[3], 0))],
            out_specs=whole((pairs // 2, sent, LANES)),
            scratch_shapes=[pltpu.VMEM((pairs // 2, sent - 8, LANES), jnp.float32)],
        ),
        out_shape=jax.ShapeDtypeStruct((pairs // 2, sent, LANES), jnp.float32),
        compiler_params=settings(),
        name="combine",
    )(info, ends, other, pars)


def prefix_kernel(end_ref, alog_ref, in_ref):
    blocks = end_ref.shape[0]
    rows = alog_ref.shape[0]
    a = [jnp.exp(alog_ref[r : r + 8, :]) * (-LOG2E) for r in range(0, rows, 8)]
    hs = [jnp.zeros((8, LANES), jnp.float32) for _ in a]
    for k in range(blocks):
        spent = end_ref[k, rows : rows + 8, :]
        for j in range(len(a)):
            in_ref[k, 8 * j : 8 * j + 8, :] = hs[j]
            hs[j] = jnp.exp2(a[j] * spent) * hs[j] + end_ref[k, 8 * j : 8 * j + 8, :]


def prefix(ends, alog):
    return pl.pallas_call(
        prefix_kernel,
        out_shape=jax.ShapeDtypeStruct((ends.shape[0], *alog.shape), jnp.float32),
        name="prefix",
    )(ends, alog)


def factor_kernel(info_ref, z_ref, out_ref):
    keep = lax.broadcasted_iota(jnp.int32, z_ref.shape, 0) < info_ref[0]
    z = z_ref[...].astype(jnp.float32)
    out_ref[...] = jnp.where(keep, z * sigmoid(z), 0.0)


def gate_factor(info, z):
    tok, chans = z.shape
    columns = pl.BlockSpec((tok, WIDE), lambda i, *_: (0, i))
    return pl.pallas_call(
        factor_kernel,
        grid_spec=pltpu.PrefetchScalarGridSpec(
            num_scalar_prefetch=1, grid=(chans // WIDE,), in_specs=[columns], out_specs=columns
        ),
        out_shape=jax.ShapeDtypeStruct((tok, chans), jnp.float32),
        compiler_params=settings(),
        name="gate_factor",
    )(info, z)


def gate_kernel(
    info_ref, y_ref, cum_ref, hin_ref, hin_too_ref, other_ref, par_ref, act_ref, factor_ref, c_ref, out_ref, y_scr, a_scr, h_scr, e_scr
):
    tok = act_ref.shape[0]
    states = a_scr.shape[0]
    a_scr[...] = jnp.exp(par_ref[VECTORS : VECTORS + states]) * (-LOG2E)
    core = info_ref[3]
    own_half = pl.program_id(0) // 4 == core

    @pl.when(own_half)
    def _():
        for q in range(ROWS // 2):
            for n in range(states):
                h_scr[n, 2 * q : 2 * q + 2, :] = hin_ref[q, 2 * n : 2 * n + 2, :]

    @pl.when(jnp.logical_not(own_half))
    def _():
        for q in range(ROWS // 2):
            for n in range(states):
                h_scr[n, 2 * q : 2 * q + 2, :] = hin_too_ref[q, 2 * n : 2 * n + 2, :]

    @pl.when(core == 1)
    def _():
        for q in range(ROWS // 2):
            for n in range(states + 1):
                e_scr[n, 2 * q : 2 * q + 2, :] = other_ref[q, 2 * n : 2 * n + 2, :]
        for n in range(states):
            h_scr[n] = jnp.exp2(a_scr[n] * e_scr[states]) * h_scr[n] + e_scr[n]

    def block(i, carry):
        for o in range(16):
            t = i * 16 + o
            cum = cum_ref[t]
            acc = [y_ref[t]] + [None] * 3
            for n in range(states):
                c = c_ref[pl.ds(n * tok + t, ROWS, stride=0), :]
                term = (c * h_scr[n]) * jnp.exp2(a_scr[n] * cum)
                acc[n % 4] = term if acc[n % 4] is None else acc[n % 4] + term
            y_scr[i * 2 + o // 8, pl.ds(o % 8, ROWS, stride=8), :] = (acc[0] + acc[1]) + (acc[2] + acc[3])
        return carry

    lax.fori_loop(0, tok // 16, block, 0)
    for g in range(ROWS):
        cols = slice(g * LANES, (g + 1) * LANES)
        y = y_scr[:, g * 8 : (g + 1) * 8, :].reshape(tok, LANES)
        direct = par_ref[6, g : g + 1, :] * act_ref[:, cols].astype(jnp.float32)
        out_ref[:, cols] = ((y + direct) * factor_ref[:, cols]).astype(jnp.bfloat16)


def gate_pass(info, y, cum, hin, hin_too, other, pars, act, factor, c_wide):
    tok, chans = act.shape
    states = c_wide.shape[0] // tok
    columns = pl.BlockSpec((tok, WIDE), lambda i, *_: (0, i))
    return pl.pallas_call(
        gate_kernel,
        grid_spec=pltpu.PrefetchScalarGridSpec(
            num_scalar_prefetch=1,
            grid=(chans // WIDE,),
            in_specs=[
                per_step(tok),
                per_step(tok),
                pl.BlockSpec((ROWS // 2, 2 * states, LANES), lambda i, *_: (i % 4, 0, 0)),
                pl.BlockSpec((ROWS // 2, 2 * states, LANES), lambda i, *_: (i % 4, 0, 0)),
                pl.BlockSpec((ROWS // 2, other.shape[1], LANES), lambda i, *_: (i, 0, 0)),
                per_step(pars.shape[0]),
                columns,
                columns,
                whole((tok * states, LANES)),
            ],
            out_specs=columns,
            scratch_shapes=[
                pltpu.VMEM((tok // 8, 8 * ROWS, LANES), jnp.float32),
                pltpu.VMEM((states, ROWS, LANES), jnp.float32),
                pltpu.VMEM((states, ROWS, LANES), jnp.float32),
                pltpu.VMEM((states + 1, ROWS, LANES), jnp.float32),
            ],
        ),
        out_shape=jax.ShapeDtypeStruct((tok, chans), jnp.bfloat16),
        compiler_params=settings(),
        name="gate_pass",
    )(info, y, cum, hin, hin_too, other, pars, act, factor, c_wide)


def device(x, y, z, core):
    return ((z & 1) * 4 + y) * 32 + x * 8 + (z >> 1) * 2 + core


def fetch(value, move):
    route = []
    for x in range(4):
        for y in range(4):
            for z in range(8):
                for core in range(2):
                    route.append((device(*move(x, y, z, core)), device(x, y, z, core)))
    return lax.ppermute(value, ("group", "ctx"), route)


def onward(axis):
    def move(x, y, z, core):
        step = 1 - 2 * core
        return ((x + step) % 4, y, z, core) if axis == "x" else (x, (y + step) % 4, z, core)

    return move


def flip(*bits):
    def move(x, y, z, core):
        z_bits = sum(bit for axis, bit in bits if axis == "z")
        core_bits = sum(bit for axis, bit in bits if axis == "core")
        return x, y, z ^ z_bits, core ^ core_bits

    return move


def four(value, low, high, own):
    at_low, at_high, at_both = fetch(value, flip(low)), fetch(value, flip(high)), fetch(value, flip(low, high))

    def pair(bit, here, there):
        zero = (own[bit[0]] & bit[1]) == 0
        return jnp.concatenate([jnp.where(zero, here, there), jnp.where(zero, there, here)], axis=0)

    return pair(high, pair(low, value, at_low), pair(low, at_high, at_both))


def farther(near, axis, own_core):
    return fetch(jnp.where(own_core == 0, near[:, :1], near[:, 1:]), onward(axis))


def swap(value):
    return fetch(value, flip(("core", 1)))


def row_of_four(value, axis, own_core):
    near = fetch(value, onward(axis))
    far = farther(near, axis, own_core)
    near_too, far_too = swap(near), swap(far)
    zero = own_core == 0
    far = jnp.concatenate([jnp.where(zero, far, far_too), jnp.where(zero, far_too, far)], axis=1)
    return jnp.concatenate([value, jnp.where(zero, near, near_too), far, jnp.where(zero, near_too, near)], axis=0)


def exchange(value):
    groups = [list(range(core, 32, 2)) for core in range(2)]
    return lax.all_to_all(value, "ctx", split_axis=0, concat_axis=0, tiled=True, axis_index_groups=groups)


def shards(
    hidden_x, gate_z, lengths, conv_weight, conv_bias, xproj_weight, dtproj_weight, dt_bias, a_log, skip_gain
):
    x, z = hidden_x[0], gate_z[0]
    tok, chans = x.shape
    taps = conv_weight.shape[0]
    rank = dtproj_weight.shape[0]
    states = a_log.shape[0]
    blocks = lax.axis_size("ctx")
    length = lengths[0]
    group, ctx = lax.axis_index("group"), lax.axis_index("ctx")
    own_x, own_y, own_core = ctx >> 3, group & 3, ctx & 1
    own_z = ((ctx >> 1) & 3) * 2 + (group >> 2)
    own = {"x": own_x, "y": own_y, "z": own_z, "core": own_core}
    info = jnp.stack([lengths[0, 0], own_x, own_y, own_core]).astype(jnp.int32)

    edge = jnp.arange(tok - (taps - 1), tok, dtype=jnp.int32)[:, None] < length
    edge = jnp.where(edge, x[tok - (taps - 1) :], jnp.bfloat16(0))
    rim = lax.ppermute(edge, "ctx", [(i, i + 1) for i in range(blocks - 1)])

    small = jnp.concatenate([conv_weight, conv_bias[None], dt_bias[None], skip_gain[None], a_log, a_log[:1]], axis=0).T
    width, count = small.shape
    high = lax.reduce_precision(small, 8, 7)
    middle = lax.reduce_precision(small - high, 8, 7)
    last = (small - high) - middle
    parts = [v.astype(jnp.bfloat16) for v in (high, middle, last)]
    fill = -(xproj_weight.shape[1] + 3 * count + rank) % LANES
    parts += [jnp.zeros((width, fill), jnp.bfloat16), dtproj_weight.T]
    mats = jnp.concatenate([xproj_weight, *parts], axis=1)[None]
    mats, rim = lax.optimization_barrier((four(mats, ("z", 4), ("z", 2), own), rim))
    mats = four(mats, ("z", 1), ("core", 1), own)
    mats = mats.reshape(1, 2, 2, 4, *mats.shape[1:])
    upper = row_of_four(mats[..., : width // 2, :], "y", own_core)
    lower = row_of_four(mats[..., width // 2 :, :], "x", own_core)
    nears = fetch(upper, onward("x")), fetch(lower, onward("y"))
    *nears, factor, rim = lax.optimization_barrier((*nears, gate_factor(info, z), rim))
    rim = jnp.concatenate([jnp.zeros((8 - (taps - 1), chans), x.dtype), rim], axis=0)
    pieces = []
    for value, near, axis in ((upper, nears[0], "x"), (lower, nears[1], "y")):
        far = farther(near, axis, own_core)
        pieces += [value, near, swap(near), far, swap(far)]

    act, pars, y, cum, ends, c_wide = scan_pass(info, x, rim, pieces, rank, states, count)
    other = swap(ends)
    chip = combine(info, ends, other, pars)
    place = 2 * ((ctx & 1) * (blocks // 2) + (ctx >> 1))
    mine = lax.dynamic_slice_in_dim(pars[VECTORS : VECTORS + states], place, 2, axis=1).reshape(2 * states, LANES)
    chip = exchange(chip)
    hin = exchange(prefix(chip, mine))
    out = gate_pass(info, y, cum, hin, swap(hin), other, pars, act, factor, c_wide)
    return out[None]


def solution(mesh):
    spread = ("group", "ctx")
    in_specs = (
        P("group", "ctx", None),
        P("group", "ctx", None),
        P("group", "ctx"),
        P(None, spread),
        P(spread),
        P(spread, None),
        P(None, spread),
        P(spread),
        P(None, spread),
        P(spread),
    )
    return jax.shard_map(
        shards, mesh=mesh, in_specs=in_specs, out_specs=P("group", "ctx", None), check_vma=False
    )
```

```python
import jax
import jax.numpy as jnp
from jax import lax
from jax.experimental import pallas as pl
from jax.experimental.pallas import tpu as pltpu
from jax.sharding import PartitionSpec as P

LOG2E = 1.4426950408889634
LANES = 128
ROWS = 8
VECTORS = 7
WIDE = ROWS * LANES


def sigmoid(v):
    return 1.0 / (1.0 + jnp.exp(-v))


def log_one_plus(u):
    w = 1.0 + u
    return jnp.log(w) + (u - (w - 1.0))


def settings():
    return pltpu.CompilerParams(dimension_semantics=("arbitrary",), vmem_limit_bytes=56 << 20)


def whole(shape):
    return pl.BlockSpec(shape, lambda i, *_: (0,) * len(shape))


def per_step(count):
    return pl.BlockSpec((count, ROWS, LANES), lambda i, *_: (0, i, 0))


def piece_specs(pieces):
    specs = []
    for k, p in enumerate(pieces):
        rest = (p.shape[1], 1, *p.shape[3:])
        if k < len(pieces) // 2:
            specs.append(
                pl.BlockSpec((1, *rest), lambda i, s: ((jnp.minimum(i, 7) - s[2]) & 3, 0, jnp.minimum(i, 7) // 4, 0, 0, 0))
            )
        else:
            specs.append(pl.BlockSpec((4, *rest), lambda i, s: (0, 0, jnp.minimum(i, 7) // 4, 0, 0, 0)))
    return specs


def assemble(step, info_ref, piece_refs, w_ref):
    own_x, own_y, own_core = info_ref[1], info_ref[2], info_ref[3]
    half = piece_refs[0].shape[4]
    many = len(piece_refs) // 2
    ahead = 1 + 2 * own_core
    away = (0, ahead, 4 - ahead, 2, 2)
    first = (0, 0, 0, own_core, 1 - own_core)
    for j, ref in enumerate(piece_refs[:many]):
        at = (own_x + away[j]) & 3
        for core in range(ref.shape[1]):
            for h in range(4):
                w_ref[at, (0, 2, 1, 3)[h], first[j] + core, 0:half, :] = ref[0, core, 0, h]
    wanted = (step - own_y) & 3
    for j, ref in enumerate(piece_refs[many:]):

        @pl.when(wanted == away[j])
        def _(ref=ref, first=first[j]):
            for q in range(4):
                for core in range(ref.shape[1]):
                    for h in range(4):
                        w_ref[(own_x + q) & 3, (0, 2, 1, 3)[h], first + core, half : 2 * half, :] = ref[q, core, 0, h]


def scan_kernel(info_ref, x_ref, rim_ref, *refs):
    *piece_refs, act_ref, par_ref, y_ref, cum_ref, end_ref, c_ref = refs[:-10]
    sum_scr, low_scr, b_scr, act_scr, par_scr, pad_scr, d_scr, x_scr, a_scr, w_scr = refs[-10:]
    step = pl.program_id(0)
    many = act_scr.shape[0]
    tok, rank = low_scr.shape
    states = a_scr.shape[0]
    keep = lax.broadcasted_iota(jnp.int32, (tok, LANES), 0) < info_ref[0]

    @pl.when(step == 0)
    def _():
        sum_scr[...] = jnp.zeros_like(sum_scr)

    @pl.when(step < many)
    def _():
        assemble(step, info_ref, piece_refs, w_scr.at[step])
        acts = []
        count = par_scr.shape[1] // ROWS
        after = rank + 2 * states
        for g in range(ROWS):
            cols = slice(g * LANES, (g + 1) * LANES)
            beside = w_scr[step, g // 2, 2 * (g % 2) : 2 * (g % 2) + 2].reshape(LANES, w_scr.shape[-1])
            beside = beside[:, after - after % LANES : after - after % LANES + LANES].astype(jnp.float32).T
            at = after % LANES
            parts = [beside[at + k * count : at + (k + 1) * count] for k in range(3)]
            vectors = (parts[0] + parts[1]) + parts[2]
            par_scr[step, pl.ds(g, count, stride=ROWS), :] = vectors
            par_ref[:, g, :] = vectors
            pad = jnp.concatenate(
                [rim_ref[:, cols].astype(jnp.float32), jnp.where(keep, x_ref[:, cols].astype(jnp.float32), 0.0)], axis=0
            )
            pad_scr[g % 2] = pad
            total = vectors[4:5] + vectors[0:1] * pad_scr[g % 2, 5 : 5 + tok, :]
            for k in range(1, 4):
                total = total + vectors[k : k + 1] * pad_scr[g % 2, 5 + k : 5 + k + tok, :]
            act = (total * sigmoid(total)).astype(jnp.bfloat16)
            act_ref[:, cols] = act
            act_scr[step, :, cols] = act
            acts.append(act)
            if g % 2:
                weight = w_scr[step, g // 2].reshape(2 * LANES, w_scr.shape[-1])[:, : sum_scr.shape[1]]
                both = jnp.concatenate(acts[-2:], axis=1)
                sum_scr[...] += jnp.dot(both, weight, preferred_element_type=jnp.float32)
        @pl.when(step == many - 1)
        def _():
            low_scr[...] = sum_scr[:, :rank].astype(jnp.bfloat16)
            for n in range(states):
                for ref, col in ((b_scr, rank + n), (c_ref, rank + states + n)):
                    ref[n * tok : (n + 1) * tok, :] = jnp.broadcast_to(sum_scr[:, col : col + 1], (tok, LANES))

    @pl.when(step >= many)
    def _():
        at = step - many
        raw = lax.dot_general(
            low_scr[...],
            w_scr[at].reshape(WIDE, w_scr.shape[-1])[:, w_scr.shape[-1] - rank :],
            (((1,), (1,)), ((), ())),
            preferred_element_type=jnp.float32,
        )
        for g in range(ROWS):
            cols = slice(g * LANES, (g + 1) * LANES)
            v = raw[:, cols] + par_scr[at, 5 * ROWS + g : 5 * ROWS + g + 1, :]
            soft = jnp.maximum(v, 0.0) + log_one_plus(jnp.exp(-jnp.abs(v)))
            d = jnp.where(keep, soft, 0.0)
            place = slice(g * 8, (g + 1) * 8)
            d_scr[:, place, :] = d.reshape(tok // 8, 8, LANES)
            dx = d * act_scr[at, :, cols].astype(jnp.float32)
            x_scr[:, place, :] = dx.reshape(tok // 8, 8, LANES)
        for n in range(states):
            row = (VECTORS + n) * ROWS
            a_scr[n] = jnp.exp(par_scr[at, row : row + ROWS, :]) * (-LOG2E)

        def block(i, carry):
            hs, cum = carry
            hs = list(hs)
            for o in range(32):
                t = i * 32 + o
                tile = i * 4 + o // 8
                d = d_scr[tile, pl.ds(o % 8, ROWS, stride=8), :]
                dx = x_scr[tile, pl.ds(o % 8, ROWS, stride=8), :]
                cum = cum + d
                acc = [None] * 4
                for n in range(states):
                    b = b_scr[pl.ds(n * tok + t, ROWS, stride=0), :]
                    c = c_ref[pl.ds(n * tok + t, ROWS, stride=0), :]
                    hs[n] = jnp.exp2(a_scr[n] * d) * hs[n] + dx * b
                    term = c * hs[n]
                    acc[n % 4] = term if acc[n % 4] is None else acc[n % 4] + term
                y_ref[t] = (acc[0] + acc[1]) + (acc[2] + acc[3])
                cum_ref[t] = cum
            return tuple(hs), cum

        zero = jnp.zeros((ROWS, LANES), jnp.float32)
        hs, cum = lax.fori_loop(0, tok // 32, block, ((zero,) * states, zero))
        for q in range(ROWS // 2):
            pair = slice(2 * q, 2 * q + 2)
            for n in range(states):
                end_ref[q, 2 * n : 2 * n + 2, :] = hs[n][pair]
            for k in range(4):
                row = 2 * states + 2 * k
                end_ref[q, row : row + 2, :] = cum[pair]


def scan_pass(info, x, rim, pieces, rank, states, count):
    tok, chans = x.shape
    rows, cols = pieces[0].shape[4:]
    many = chans // WIDE
    groups = chans // LANES
    sent = 2 * states + 8

    def turn(shape, where):
        def index(i, s):
            later = jnp.maximum(i - many, 0)
            return (0,) * where + (later,) + (0,) * (len(shape) - 1 - where)

        return pl.BlockSpec(shape, index)

    return pl.pallas_call(
        scan_kernel,
        grid_spec=pltpu.PrefetchScalarGridSpec(
            num_scalar_prefetch=1,
            grid=(2 * many,),
            in_specs=[
                pl.BlockSpec((tok, WIDE), lambda i, s: (0, jnp.minimum(i, many - 1))),
                pl.BlockSpec((8, WIDE), lambda i, s: (0, jnp.minimum(i, many - 1))),
                *piece_specs(pieces),
            ],
            out_specs=[
                pl.BlockSpec((tok, WIDE), lambda i, s: (0, jnp.minimum(i, many - 1))),
                pl.BlockSpec((count, ROWS, LANES), lambda i, s: (0, jnp.minimum(i, many - 1), 0)),
                turn((tok, ROWS, LANES), 1),
                turn((tok, ROWS, LANES), 1),
                turn((ROWS // 2, sent, LANES), 0),
                whole((tok * states, LANES)),
            ],
            scratch_shapes=[
                pltpu.VMEM((tok, cols - rank), jnp.float32),
                pltpu.VMEM((tok, rank), jnp.bfloat16),
                pltpu.VMEM((tok * states, LANES), jnp.float32),
                pltpu.VMEM((many, tok, WIDE), jnp.bfloat16),
                pltpu.VMEM((many, count * ROWS, LANES), jnp.float32),
                pltpu.VMEM((2, tok + 8, LANES), jnp.float32),
                pltpu.VMEM((tok // 8, 8 * ROWS, LANES), jnp.float32),
                pltpu.VMEM((tok // 8, 8 * ROWS, LANES), jnp.float32),
                pltpu.VMEM((states, ROWS, LANES), jnp.float32),
                pltpu.VMEM((many, 4, 4, 2, 2 * rows, cols), jnp.bfloat16),
            ],
        ),
        out_shape=[
            jax.ShapeDtypeStruct((tok, chans), jnp.bfloat16),
            jax.ShapeDtypeStruct((count, groups, LANES), jnp.float32),
            jax.ShapeDtypeStruct((tok, groups, LANES), jnp.float32),
            jax.ShapeDtypeStruct((tok, groups, LANES), jnp.float32),
            jax.ShapeDtypeStruct((groups // 2, sent, LANES), jnp.float32),
            jax.ShapeDtypeStruct((tok * states, LANES), jnp.float32),
        ],
        compiler_params=settings(),
        name="scan_pass",
    )(info, x, rim, *pieces)


def combine_kernel(info_ref, ends_ref, other_ref, par_ref, out_ref, a_scr):
    pairs, sent, _ = out_ref.shape
    rows = sent - 8
    for p in range(pairs):
        for n in range(rows // 2):
            a_scr[p, 2 * n : 2 * n + 2, :] = par_ref[VECTORS + n, 2 * p : 2 * p + 2, :]
    earlier = info_ref[3] == 0
    for p in range(pairs):
        own, other = ends_ref[p], other_ref[p]
        head, tail = jnp.where(earlier, own, other), jnp.where(earlier, other, own)
        spent = tail[rows:]
        for r in range(0, rows, 8):
            decay = jnp.exp2(jnp.exp(a_scr[p, r : r + 8, :]) * (-LOG2E) * spent)
            out_ref[p, r : r + 8, :] = decay * head[r : r + 8] + tail[r : r + 8]
        out_ref[p, rows:, :] = head[rows:] + spent


def combine(info, ends, other, pars):
    pairs, sent, _ = ends.shape
    half = pl.BlockSpec((pairs // 2, sent, LANES), lambda i, s: (s[3], 0, 0))
    return pl.pallas_call(
        combine_kernel,
        grid_spec=pltpu.PrefetchScalarGridSpec(
            num_scalar_prefetch=1,
            grid=(1,),
            in_specs=[half, half, pl.BlockSpec((pars.shape[0], pairs, LANES), lambda i, s: (0, s[3], 0))],
            out_specs=whole((pairs // 2, sent, LANES)),
            scratch_shapes=[pltpu.VMEM((pairs // 2, sent - 8, LANES), jnp.float32)],
        ),
        out_shape=jax.ShapeDtypeStruct((pairs // 2, sent, LANES), jnp.float32),
        compiler_params=settings(),
        name="combine",
    )(info, ends, other, pars)


def prefix_kernel(end_ref, alog_ref, in_ref):
    blocks = end_ref.shape[0]
    rows = alog_ref.shape[0]
    a = [jnp.exp(alog_ref[r : r + 8, :]) * (-LOG2E) for r in range(0, rows, 8)]
    hs = [jnp.zeros((8, LANES), jnp.float32) for _ in a]
    for k in range(blocks):
        spent = end_ref[k, rows : rows + 8, :]
        for j in range(len(a)):
            in_ref[k, 8 * j : 8 * j + 8, :] = hs[j]
            hs[j] = jnp.exp2(a[j] * spent) * hs[j] + end_ref[k, 8 * j : 8 * j + 8, :]


def prefix(ends, alog):
    return pl.pallas_call(
        prefix_kernel,
        out_shape=jax.ShapeDtypeStruct((ends.shape[0], *alog.shape), jnp.float32),
        name="prefix",
    )(ends, alog)


def factor_kernel(info_ref, z_ref, out_ref):
    keep = lax.broadcasted_iota(jnp.int32, z_ref.shape, 0) < info_ref[0]
    z = z_ref[...].astype(jnp.float32)
    out_ref[...] = jnp.where(keep, z * sigmoid(z), 0.0)


def gate_factor(info, z):
    tok, chans = z.shape
    columns = pl.BlockSpec((tok, WIDE), lambda i, *_: (0, i))
    return pl.pallas_call(
        factor_kernel,
        grid_spec=pltpu.PrefetchScalarGridSpec(
            num_scalar_prefetch=1, grid=(chans // WIDE,), in_specs=[columns], out_specs=columns
        ),
        out_shape=jax.ShapeDtypeStruct((tok, chans), jnp.float32),
        compiler_params=settings(),
        name="gate_factor",
    )(info, z)


def gate_kernel(
    info_ref, y_ref, cum_ref, hin_ref, hin_too_ref, other_ref, par_ref, act_ref, factor_ref, c_ref, out_ref, y_scr, a_scr, h_scr, e_scr
):
    tok = act_ref.shape[0]
    states = a_scr.shape[0]
    a_scr[...] = jnp.exp(par_ref[VECTORS : VECTORS + states]) * (-LOG2E)
    core = info_ref[3]
    own_half = pl.program_id(0) // 4 == core

    @pl.when(own_half)
    def _():
        for q in range(ROWS // 2):
            for n in range(states):
                h_scr[n, 2 * q : 2 * q + 2, :] = hin_ref[q, 2 * n : 2 * n + 2, :]

    @pl.when(jnp.logical_not(own_half))
    def _():
        for q in range(ROWS // 2):
            for n in range(states):
                h_scr[n, 2 * q : 2 * q + 2, :] = hin_too_ref[q, 2 * n : 2 * n + 2, :]

    @pl.when(core == 1)
    def _():
        for q in range(ROWS // 2):
            for n in range(states + 1):
                e_scr[n, 2 * q : 2 * q + 2, :] = other_ref[q, 2 * n : 2 * n + 2, :]
        for n in range(states):
            h_scr[n] = jnp.exp2(a_scr[n] * e_scr[states]) * h_scr[n] + e_scr[n]

    def block(i, carry):
        for o in range(32):
            t = i * 32 + o
            cum = cum_ref[t]
            acc = [y_ref[t]] + [None] * 3
            for n in range(states):
                c = c_ref[pl.ds(n * tok + t, ROWS, stride=0), :]
                term = (c * h_scr[n]) * jnp.exp2(a_scr[n] * cum)
                acc[n % 4] = term if acc[n % 4] is None else acc[n % 4] + term
            y_scr[i * 4 + o // 8, pl.ds(o % 8, ROWS, stride=8), :] = (acc[0] + acc[1]) + (acc[2] + acc[3])
        return carry

    lax.fori_loop(0, tok // 32, block, 0)
    for g in range(ROWS):
        cols = slice(g * LANES, (g + 1) * LANES)
        y = y_scr[:, g * 8 : (g + 1) * 8, :].reshape(tok, LANES)
        direct = par_ref[6, g : g + 1, :] * act_ref[:, cols].astype(jnp.float32)
        out_ref[:, cols] = ((y + direct) * factor_ref[:, cols]).astype(jnp.bfloat16)


def gate_pass(info, y, cum, hin, hin_too, other, pars, act, factor, c_wide):
    tok, chans = act.shape
    states = c_wide.shape[0] // tok
    columns = pl.BlockSpec((tok, WIDE), lambda i, *_: (0, i))
    return pl.pallas_call(
        gate_kernel,
        grid_spec=pltpu.PrefetchScalarGridSpec(
            num_scalar_prefetch=1,
            grid=(chans // WIDE,),
            in_specs=[
                per_step(tok),
                per_step(tok),
                pl.BlockSpec((ROWS // 2, 2 * states, LANES), lambda i, *_: (i % 4, 0, 0)),
                pl.BlockSpec((ROWS // 2, 2 * states, LANES), lambda i, *_: (i % 4, 0, 0)),
                pl.BlockSpec((ROWS // 2, other.shape[1], LANES), lambda i, *_: (i, 0, 0)),
                per_step(pars.shape[0]),
                columns,
                columns,
                whole((tok * states, LANES)),
            ],
            out_specs=columns,
            scratch_shapes=[
                pltpu.VMEM((tok // 8, 8 * ROWS, LANES), jnp.float32),
                pltpu.VMEM((states, ROWS, LANES), jnp.float32),
                pltpu.VMEM((states, ROWS, LANES), jnp.float32),
                pltpu.VMEM((states + 1, ROWS, LANES), jnp.float32),
            ],
        ),
        out_shape=jax.ShapeDtypeStruct((tok, chans), jnp.bfloat16),
        compiler_params=settings(),
        name="gate_pass",
    )(info, y, cum, hin, hin_too, other, pars, act, factor, c_wide)


def device(x, y, z, core):
    return ((z & 1) * 4 + y) * 32 + x * 8 + (z >> 1) * 2 + core


def fetch(value, move):
    route = []
    for x in range(4):
        for y in range(4):
            for z in range(8):
                for core in range(2):
                    route.append((device(*move(x, y, z, core)), device(x, y, z, core)))
    return lax.ppermute(value, ("group", "ctx"), route)


def onward(axis):
    def move(x, y, z, core):
        step = 1 - 2 * core
        return ((x + step) % 4, y, z, core) if axis == "x" else (x, (y + step) % 4, z, core)

    return move


def flip(*bits):
    def move(x, y, z, core):
        z_bits = sum(bit for axis, bit in bits if axis == "z")
        core_bits = sum(bit for axis, bit in bits if axis == "core")
        return x, y, z ^ z_bits, core ^ core_bits

    return move


def four(value, low, high, own):
    at_low, at_high, at_both = fetch(value, flip(low)), fetch(value, flip(high)), fetch(value, flip(low, high))

    def pair(bit, here, there):
        zero = (own[bit[0]] & bit[1]) == 0
        return jnp.concatenate([jnp.where(zero, here, there), jnp.where(zero, there, here)], axis=0)

    return pair(high, pair(low, value, at_low), pair(low, at_high, at_both))


def farther(near, axis, own_core):
    return fetch(jnp.where(own_core == 0, near[:, :1], near[:, 1:]), onward(axis))


def swap(value):
    return fetch(value, flip(("core", 1)))


def row_of_four(value, axis, own_core):
    near = fetch(value, onward(axis))
    far = farther(near, axis, own_core)
    near_too, far_too = swap(near), swap(far)
    zero = own_core == 0
    far = jnp.concatenate([jnp.where(zero, far, far_too), jnp.where(zero, far_too, far)], axis=1)
    return jnp.concatenate([value, jnp.where(zero, near, near_too), far, jnp.where(zero, near_too, near)], axis=0)


def exchange(value):
    groups = [list(range(core, 32, 2)) for core in range(2)]
    return lax.all_to_all(value, "ctx", split_axis=0, concat_axis=0, tiled=True, axis_index_groups=groups)


def shards(
    hidden_x, gate_z, lengths, conv_weight, conv_bias, xproj_weight, dtproj_weight, dt_bias, a_log, skip_gain
):
    x, z = hidden_x[0], gate_z[0]
    tok, chans = x.shape
    taps = conv_weight.shape[0]
    rank = dtproj_weight.shape[0]
    states = a_log.shape[0]
    blocks = lax.axis_size("ctx")
    length = lengths[0]
    group, ctx = lax.axis_index("group"), lax.axis_index("ctx")
    own_x, own_y, own_core = ctx >> 3, group & 3, ctx & 1
    own_z = ((ctx >> 1) & 3) * 2 + (group >> 2)
    own = {"x": own_x, "y": own_y, "z": own_z, "core": own_core}
    info = jnp.stack([lengths[0, 0], own_x, own_y, own_core]).astype(jnp.int32)

    edge = jnp.arange(tok - (taps - 1), tok, dtype=jnp.int32)[:, None] < length
    edge = jnp.where(edge, x[tok - (taps - 1) :], jnp.bfloat16(0))
    rim = lax.ppermute(edge, "ctx", [(i, i + 1) for i in range(blocks - 1)])

    small = jnp.concatenate([conv_weight, conv_bias[None], dt_bias[None], skip_gain[None], a_log, a_log[:1]], axis=0).T
    width, count = small.shape
    high = lax.reduce_precision(small, 8, 7)
    middle = lax.reduce_precision(small - high, 8, 7)
    last = (small - high) - middle
    parts = [v.astype(jnp.bfloat16) for v in (high, middle, last)]
    fill = -(xproj_weight.shape[1] + 3 * count + rank) % LANES
    parts += [jnp.zeros((width, fill), jnp.bfloat16), dtproj_weight.T]
    mats = jnp.concatenate([xproj_weight, *parts], axis=1)[None]
    mats, rim = lax.optimization_barrier((four(mats, ("z", 4), ("z", 2), own), rim))
    mats = four(mats, ("z", 1), ("core", 1), own)
    mats = mats.reshape(1, 2, 2, 4, *mats.shape[1:])
    upper = row_of_four(mats[..., : width // 2, :], "y", own_core)
    lower = row_of_four(mats[..., width // 2 :, :], "x", own_core)
    nears = fetch(upper, onward("x")), fetch(lower, onward("y"))
    *nears, factor, rim = lax.optimization_barrier((*nears, gate_factor(info, z), rim))
    rim = jnp.concatenate([jnp.zeros((8 - (taps - 1), chans), x.dtype), rim], axis=0)
    pieces = []
    for value, near, axis in ((upper, nears[0], "x"), (lower, nears[1], "y")):
        far = farther(near, axis, own_core)
        pieces += [value, near, swap(near), far, swap(far)]

    act, pars, y, cum, ends, c_wide = scan_pass(info, x, rim, pieces, rank, states, count)
    other = swap(ends)
    chip = combine(info, ends, other, pars)
    place = 2 * ((ctx & 1) * (blocks // 2) + (ctx >> 1))
    mine = lax.dynamic_slice_in_dim(pars[VECTORS : VECTORS + states], place, 2, axis=1).reshape(2 * states, LANES)
    chip = exchange(chip)
    hin = exchange(prefix(chip, mine))
    out = gate_pass(info, y, cum, hin, swap(hin), other, pars, act, factor, c_wide)
    return out[None]


def solution(mesh):
    spread = ("group", "ctx")
    in_specs = (
        P("group", "ctx", None),
        P("group", "ctx", None),
        P("group", "ctx"),
        P(None, spread),
        P(spread),
        P(spread, None),
        P(None, spread),
        P(spread),
        P(None, spread),
        P(spread),
    )
    return jax.shard_map(
        shards, mesh=mesh, in_specs=in_specs, out_specs=P("group", "ctx", None), check_vma=False
    )
```
